32 devices in a mesh: groups: 2 (over y), gx: 4 (over z), gy: 2 (over x), col: 2 (over core).
Axes of the slice: x: 2, y: 2, z: 4, core: 2. Of those that a mesh axis runs over, the one named last changes fastest.
Arguments:
- volume: bfloat16 [32, 16, 2048], P(('groups', 'gx'), ('gy', 'col')), parts along dimension 0, may hold values from -6 to 6
- fine_kernel: bfloat16 [27, 64, 64], replicated, may hold values from -0.15625 to 0.15625
- fine_bias: float32 [64], replicated, may hold values from -3 to 3
- down_kernel: bfloat16 [512, 512], replicated, may hold values from -0.25 to 0.25
- down_bias: float32 [512], replicated, may hold values from -3 to 3
- bottle_kernel: bfloat16 [27, 512, 1024], P(None, None, 'gx'), may hold values from -0.0546875 to 0.0546875
- bottle_bias: float32 [1024], P('gx'), may hold values from -3 to 3
- up_kernel: bfloat16 [1024, 512], replicated, may hold values from -0.1875 to 0.1875
- up_bias: float32 [64], replicated, may hold values from -3 to 3
Outputs:
- decoded: bfloat16 [32, 16, 2048], P(('groups', 'gx'), ('gy', 'col')), parts along dimension 0
The draws below stay inside these ranges and needn't reach their ends.
There are 2 independent parts, one for each index of `groups`. The reference program is written for one: setup_inputs(seed, part) draws one part's arguments, and reference() takes and returns one part's arrays. A program takes and returns all parts, laid end to end along the dimension named above; an argument that names none is the same for every part. Nothing has to cross between parts.
All inputs are finite; a program needn't handle non-finite values.
Results may differ from the reference program's by a relative error of at most 0.0047.
Values may be sent and summed in bfloat16 or wider, within the bound.
A program may use at most 128 MiB of HBM per device.

```python
import jax
import jax.numpy as jnp

C = 64
CD = 512
CB = 1024
NZ = 32
NX = 16
NY = 16


def levels(key, shape, pieces, least, largest):
    factor_of = 1.0
    for position, parts in pieces:
        steps = jax.random.uniform(jax.random.fold_in(jax.random.fold_in(key, 6), position), (parts,), jnp.float32, least / len(pieces), largest / len(pieces))
        factor_of = factor_of * jnp.repeat(jnp.exp(steps), shape[position] // parts).reshape((-1,) + (1,) * (len(shape) - 1 - position))
    return factor_of


def normal_values(key, dims, deviation, limit, cuts=(), kind=jnp.bfloat16):
    result = deviation * jax.random.normal(key, dims, jnp.float32)
    if cuts:
        result = result * levels(key, dims, cuts, -0.22, 0.18)
    return jnp.clip(result, -limit, limit).astype(kind)


def setup_inputs(seed: int = 0, part: int = 0) -> dict:
    splits = jax.random.split(jax.random.key(seed), 10)
    part_splits = jax.random.split(jax.random.fold_in(splits[9], part), 10)
    volume = normal_values(part_splits[0], (NX, NY, NZ * C), 1.0, 6.0, ((0, 4), (1, 4)))
    fine_kernel = normal_values(splits[1], (27, C, C), (27 * C) ** -0.5, 0.15625)
    fine_bias = normal_values(splits[2], (C,), 0.5, 3.0, (), jnp.float32)
    down_kernel = normal_values(splits[3], (8 * C, CD), (8 * C) ** -0.5, 0.25)
    down_bias = normal_values(splits[4], (CD,), 0.5, 3.0, (), jnp.float32)
    bottle_kernel = normal_values(splits[5], (27, CD, CB), (27 * CD) ** -0.5, 0.0546875, ((2, 4),))
    bottle_bias = normal_values(splits[6], (CB,), 0.5, 3.0, ((0, 4),), jnp.float32)
    up_kernel = normal_values(splits[7], (CB, 8 * C), CB ** -0.5, 0.1875)
    up_bias = normal_values(splits[8], (C,), 0.5, 3.0, (), jnp.float32)
    return dict(volume=volume, fine_kernel=fine_kernel, fine_bias=fine_bias, down_kernel=down_kernel, down_bias=down_bias, bottle_kernel=bottle_kernel, bottle_bias=bottle_bias, up_kernel=up_kernel, up_bias=up_bias)


def conv_three(padded, kernel, bias, nx, ny, nz):
    chans = padded.shape[3]
    total = jnp.zeros((nx * ny * nz, kernel.shape[2]), jnp.float32)
    for i in range(3):
        for j in range(3):
            for k in range(3):
                piece = padded[i:i + nx, j:j + ny, k:k + nz, :].reshape(nx * ny * nz, chans)
                total = total + jnp.dot(piece, kernel[i * 9 + j * 3 + k], preferred_element_type=jnp.float32)
    return (total + bias[None, :]).reshape(nx, ny, nz, kernel.shape[2])


def reference(volume, fine_kernel, fine_bias, down_kernel, down_bias, bottle_kernel, bottle_bias, up_kernel, up_bias):
    cells = volume.reshape(NX, NY, NZ, C)
    padded = jnp.pad(cells, ((1, 1), (1, 1), (1, 1), (0, 0)))
    fine = jax.nn.silu(conv_three(padded, fine_kernel, fine_bias, NX, NY, NZ)).astype(jnp.bfloat16)
    hx, hy, hz = NX // 2, NY // 2, NZ // 2
    blocks = fine.reshape(hx, 2, hy, 2, hz, 2, C).transpose(0, 2, 4, 1, 3, 5, 6).reshape(hx * hy * hz, 8 * C)
    coarse = jax.nn.silu(jnp.dot(blocks, down_kernel, preferred_element_type=jnp.float32) + down_bias[None, :]).astype(jnp.bfloat16)
    coarse = coarse.reshape(hx, hy, hz, CD)
    cpad = jnp.pad(coarse, ((1, 1), (1, 1), (1, 1), (0, 0)))
    bottle = jax.nn.silu(conv_three(cpad, bottle_kernel, bottle_bias, hx, hy, hz)).astype(jnp.bfloat16)
    lifted = jnp.dot(bottle.reshape(hx * hy * hz, CB), up_kernel, preferred_element_type=jnp.float32)
    lifted = lifted.reshape(hx, hy, hz, 8, C) + up_bias[None, None, None, None, :]
    lifted = lifted.reshape(hx, hy, hz, 2, 2, 2, C).transpose(0, 3, 1, 4, 2, 5, 6).reshape(NX, NY, NZ, C)
    decoded = (fine.astype(jnp.float32) + lifted).astype(jnp.bfloat16)
    return decoded.reshape(NX, NY, NZ * C)
```

```python
import functools

import jax
import jax.numpy as jnp
from jax import lax
from jax.experimental import pallas as pl
from jax.experimental.pallas import tpu as pltpu
from jax.sharding import PartitionSpec as P

MESH = pl.DeviceIdType.MESH
F32 = jnp.float32
BF16 = jnp.bfloat16


def silu(a):
    return (0.5 * a) * (1.0 + jnp.tanh(0.5 * a))


def shifted(a, amount, depth):
    rows = a.shape[0]
    z = lax.broadcasted_iota(jnp.int32, a.shape, 0) % depth
    moved = pltpu.roll(a, amount % rows, 0)
    keep = z >= amount if amount > 0 else z < depth + amount
    return jnp.where(keep, moved, 0.0)


def body(
    sizes,
    vol_hbm,
    fk_hbm,
    fb_hbm,
    dk_hbm,
    db_hbm,
    bk_hbm,
    bb_hbm,
    uk_hbm,
    ub_hbm,
    out_ref,
    raw,
    brick,
    fk,
    band,
    dk,
    bk,
    uk,
    fb_ref,
    db_ref,
    bb_ref,
    ub_ref,
    fine_ref,
    strip,
    acc,
    sent,
    back,
    load_sem,
    halo_send,
    halo_recv,
    edge_send,
    edge_recv,
    rest_send,
    rest_recv,
    outer_send,
    outer_recv,
    inner_send,
    inner_recv,
    swap_send,
    swap_recv,
):
    ngx, ngy, ncol = sizes
    nq = ngy * ncol
    cx, cy, depth, pair = fine_ref.shape
    chans = pair // 2
    hx, hy = cx // 2, cy // 2
    cd = dk.shape[1]
    cb = bk.shape[2]
    g = lax.axis_index("gx")
    col = lax.axis_index("col")
    q = lax.axis_index("gy") * ncol + col

    def device(gg, qq):
        return {"gx": gg, "gy": qq // ncol, "col": qq % ncol}

    loads = [
        pltpu.make_async_copy(src, dst, load_sem.at[n])
        for n, (src, dst) in enumerate(
            (
                (vol_hbm, raw),
                (fk_hbm, fk),
                (fb_hbm, fb_ref),
                (dk_hbm, dk),
                (db_hbm, db_ref),
                (bb_hbm, bb_ref),
                (uk_hbm, uk),
                (ub_hbm, ub_ref),
            )
            + tuple((bk_hbm.at[pl.ds(3 * n, 3)], bk.at[pl.ds(3 * n, 3)]) for n in range(9))
        )
    ]
    for load in loads:
        load.start()

    brick[0] = jnp.zeros_like(brick[0])
    brick[cx + 1] = jnp.zeros_like(brick[0])
    for y in (0, cy + 1):
        brick[1 : cx + 1, y] = jnp.zeros((cx, depth, pair), BF16)
    strip[0] = jnp.zeros_like(strip[0])
    strip[ngx * hx + 1] = jnp.zeros_like(strip[0])

    @pl.when(q == 0)
    def _():
        strip[1 : ngx * hx + 1, 0] = jnp.zeros((ngx * hx, depth, cd), BF16)

    @pl.when(q == nq - 1)
    def _():
        strip[1 : ngx * hx + 1, hy + 1] = jnp.zeros((ngx * hx, depth, cd), BF16)

    def valid(gg, qq):
        ok = jnp.logical_and(gg >= 0, gg < ngx)
        return jnp.logical_and(ok, jnp.logical_and(qq >= 0, qq < nq))

    barrier = pltpu.get_barrier_semaphore()

    def greet(gg, qq):
        pl.semaphore_signal(barrier, inc=1, device_id=device(gg, qq), device_id_type=MESH)

    partners = ngx - 1
    for d in range(1, ngx):
        greet(lax.rem(g + d, ngx), q)
    for b in (-1, 1):
        there = valid(g, q + b)
        partners += jnp.where(there, ngx, 0)

        @pl.when(there)
        def _():
            for d in range(ngx):
                greet(lax.rem(g + d, ngx), q + b)

    loads[0].wait()
    for x in range(cx):
        brick[1 + x, 1 : cy + 1] = (
            raw[x].astype(F32).reshape(cy, depth, pair).astype(BF16)
        )
    pl.semaphore_wait(barrier, partners)

    def remote(src, dst, send, recv, gg, qq):
        return pltpu.make_async_remote_copy(
            src_ref=src,
            dst_ref=dst,
            send_sem=send,
            recv_sem=recv,
            device_id=device(gg, qq),
            device_id_type=MESH,
        )

    def edges(step, count):
        if step == 0:
            return pl.ds(1, count), pl.ds(1, count)
        if step > 0:
            return pl.ds(count, 1), pl.ds(0, 1)
        return pl.ds(1, 1), pl.ds(count + 1, 1)

    halos = []
    for a in (-1, 0, 1):
        for b in (-1, 0, 1):
            if a == 0 and b == 0:
                continue
            t = len(halos)
            sx, dx = edges(a, cx)
            sy, dy = edges(b, cy)
            halos.append(
                (
                    valid(g + a, q + b),
                    remote(
                        brick.at[sx, sy], brick.at[dx, dy],
                        halo_send.at[t], halo_recv.at[t], g + a, q + b,
                    ),
                    valid(g - a, q - b),
                    remote(
                        brick.at[dx, dy], brick.at[dx, dy],
                        halo_send.at[t], halo_recv.at[t], g - a, q - b,
                    ),
                )
            )
    for ok, out, _, _ in halos:
        pl.when(ok)(out.start)

    loads[1].wait()
    empty = jnp.zeros((chans, chans), BF16)
    for ij in range(9):
        f0, f1, f2 = fk[3 * ij], fk[3 * ij + 1], fk[3 * ij + 2]
        band[ij * pair : ij * pair + chans] = jnp.concatenate([f1, f0, empty, f2], axis=1)
        band[ij * pair + chans : (ij + 1) * pair] = jnp.concatenate([f2, f1, f0, empty], axis=1)

    for _, _, ok, into in halos:
        pl.when(ok)(into.wait_recv)

    pieces = [
        brick[i : i + cx, j : j + cy].reshape(cx * cy * depth, pair)
        for i in range(3)
        for j in range(3)
    ]
    loads[2].wait()
    prod = jnp.dot(jnp.concatenate(pieces, axis=1), band[...], preferred_element_type=F32)
    side = prod[:, pair:]
    lane = lax.broadcasted_iota(jnp.int32, side.shape, 1)
    fb = fb_ref[...]
    total = (
        prod[:, :pair]
        + jnp.where(lane < chans, shifted(side, 1, depth), shifted(side, -1, depth))
        + jnp.concatenate([fb, fb], axis=1)
    )
    fine_ref[...] = silu(total).astype(BF16).reshape(cx, cy, depth, pair)

    loads[3].wait()
    loads[4].wait()
    cells = []
    for x in range(hx):
        for y in range(hy):
            cells.append(
                jnp.concatenate(
                    [fine_ref[2 * x + dx, 2 * y + dy] for dx in (0, 1) for dy in (0, 1)], axis=1
                )
            )
    coarse = jnp.dot(jnp.concatenate(cells, axis=0), dk[...], preferred_element_type=F32)
    coarse = silu(coarse + db_ref[...]).astype(BF16)
    strip[pl.ds(1 + hx * g, hx), 1 : hy + 1] = coarse.reshape(hx, hy, depth, cd)

    def planes(at):
        return pl.ds(1 + hx * at, hx)

    inner = 1 - 2 * col
    inner_row = 1 + jnp.where(inner > 0, hy - 1, 0)
    outer_row = 1 + jnp.where(inner > 0, 0, hy - 1)
    rest_row = 1 + jnp.where(inner > 0, 0, 1)
    inner_rim = jnp.where(inner > 0, 0, hy + 1)
    outer_rim = jnp.where(inner > 0, hy + 1, 0)
    mate = q + inner
    beyond = q - inner
    has_beyond = valid(g, beyond)

    def edge_block(source, to):
        ref = strip.at[planes(source), pl.ds(inner_row, 1)]
        return remote(ref, ref, edge_send.at[to], edge_recv.at[source], to, q)

    def rest_block(source, to):
        ref = strip.at[planes(source), pl.ds(rest_row, hy - 1)]
        return remote(ref, ref, rest_send.at[to], rest_recv.at[source], to, q)

    def outer_out(to):
        return remote(
            strip.at[planes(g), pl.ds(outer_row, 1)], strip.at[planes(g), pl.ds(outer_rim, 1)],
            outer_send.at[to], outer_recv.at[g], to, beyond,
        )

    def outer_in(source):
        ref = strip.at[planes(source), pl.ds(inner_rim, 1)]
        return remote(ref, ref, outer_send.at[source], outer_recv.at[source], source, beyond)

    def inner_out(source):
        return remote(
            strip.at[planes(source), pl.ds(inner_row, 1)], strip.at[planes(source), pl.ds(inner_rim, 1)],
            inner_send.at[source], inner_recv.at[source], g, mate,
        )

    def inner_in(source):
        ref = strip.at[planes(source), pl.ds(outer_rim, 1)]
        return remote(ref, ref, inner_send.at[source], inner_recv.at[source], g, mate)

    def others(visit, order):
        for d in order:
            for p in (g + d, g - d):
                pl.when(valid(p, q))(functools.partial(visit, p))

    near = tuple(range(1, ngx))
    far = near[::-1]

    def first_rows(p):
        pl.when(has_beyond)(outer_out(p).start)
        edge_block(g, p).start()

    others(first_rows, far)
    others(lambda p: rest_block(g, p).start(), far)
    pl.when(has_beyond)(outer_out(g).start)
    inner_out(g).start()
    for load in loads[5:]:
        load.wait()

    def forward(p):
        edge_block(p, p).wait_recv()
        inner_out(p).start()

    others(forward, near)

    def swap(to, source):
        return remote(sent.at[to], back.at[source], swap_send.at[to], swap_recv.at[source], to, q)

    rows = hx * hy * depth

    @pl.loop(0, ngx - 1)
    def _(n):
        step = jnp.where(n % 2 == 1, (n + 1) // 2, -((n + 1) // 2))
        at = g // 2 + step

        @pl.when(jnp.logical_and(at >= 0, at < ngx // 2))
        def _():
            low = jnp.where(step > 0, 2 * at + 1, 2 * at - 1)
            high = jnp.where(step < 0, 2 * at, 2 * at + 2)

            def arrived(i):
                source = low + i
                return jnp.logical_and(source <= high, valid(source, q)), source

            def bodies(i):
                ok, source = arrived(i)

                @pl.when(jnp.logical_and(ok, source != g))
                def _():
                    rest_block(source, source).wait_recv()

            def rims(i):
                ok, source = arrived(i)

                @pl.when(ok)
                def _():
                    inner_in(source).wait_recv()
                    pl.when(has_beyond)(outer_in(source).wait_recv)

            def taps(j, k):
                return sum(
                    jnp.dot(
                        strip[pl.ds(2 * hx * at + i, 2 * hx), j : j + hy].reshape(2 * rows, cd),
                        bk[9 * i + 3 * j + k],
                        preferred_element_type=F32,
                    )
                    for i in range(3)
                )

            for i in range(4):
                bodies(i)
            for k in range(3):
                acc[k] = taps(1, k)
            for i in range(4):
                rims(i)
            for k in range(3):
                acc[k] += taps(0, k) + taps(2, k)
            bottle = acc[1] + shifted(acc[0], 1, depth) + shifted(acc[2], -1, depth)
            bottle = silu(bottle + bb_ref[...]).astype(BF16)
            for i in range(2):
                p = 2 * at + i
                sent[p] = bottle[i * rows : (i + 1) * rows]
                pl.when(p != g)(swap(p, g).start)

    lifted = jnp.dot(sent[g], uk[g], preferred_element_type=F32)
    for d in range(1, ngx):
        source = lax.rem(g + d, ngx)
        swap(source, source).wait_recv()
        lifted += jnp.dot(back[source], uk[source], preferred_element_type=F32)
    ub = ub_ref[...]
    ub = jnp.concatenate([ub, ub], axis=1)
    for x in range(hx):
        for dx in (0, 1):
            columns = []
            for y in range(hy):
                at = (x * hy + y) * depth
                for dy in (0, 1):
                    c = (2 * dx + dy) * pair
                    columns.append(
                        fine_ref[2 * x + dx, 2 * y + dy].astype(F32)
                        + (lifted[at : at + depth, c : c + pair] + ub)
                    )
            whole = jnp.stack(columns).reshape(cy, depth * pair)
            out_ref[2 * x + dx] = whole.astype(BF16)

    for ok, out, _, _ in halos:
        pl.when(ok)(out.wait_send)

    def left(p):
        edge_block(g, p).wait_send()
        rest_block(g, p).wait_send()
        swap(p, g).wait_send()

    others(left, near)
    for p in range(ngx):
        pl.when(has_beyond)(outer_out(p).wait_send)
        inner_out(p).wait_send()


def local(
    sizes,
    volume,
    fine_kernel,
    fine_bias,
    down_kernel,
    down_bias,
    bottle_kernel,
    bottle_bias,
    up_kernel,
    up_bias,
):
    ngx = sizes[0]
    cx, cy, merged = volume.shape
    chans = fine_kernel.shape[1]
    pair = 2 * chans
    depth = merged // pair
    hx, hy = cx // 2, cy // 2
    cd = down_kernel.shape[1]
    cb = bottle_kernel.shape[2]
    cells = hx * hy * depth
    hbm = pl.BlockSpec(memory_space=pltpu.HBM)
    vmem = pl.BlockSpec(memory_space=pltpu.VMEM)
    dma = pltpu.SemaphoreType.DMA
    call = pl.pallas_call(
        functools.partial(body, sizes),
        out_shape=jax.ShapeDtypeStruct((cx, cy, merged), BF16),
        in_specs=[hbm] * 9,
        out_specs=vmem,
        scratch_shapes=[
            pltpu.VMEM(volume.shape, BF16),
            pltpu.VMEM((cx + 2, cy + 2, depth, pair), BF16),
            pltpu.VMEM(fine_kernel.shape, BF16),
            pltpu.VMEM((9 * pair, 2 * pair), BF16),
            pltpu.VMEM(down_kernel.shape, BF16),
            pltpu.VMEM(bottle_kernel.shape, BF16),
            pltpu.VMEM((ngx, cb, up_kernel.shape[1]), BF16),
            pltpu.VMEM((1, chans), F32),
            pltpu.VMEM((1, cd), F32),
            pltpu.VMEM((1, cb), F32),
            pltpu.VMEM((1, chans), F32),
            pltpu.VMEM((cx, cy, depth, pair), BF16),
            pltpu.VMEM((ngx * hx + 2, hy + 2, depth, cd), BF16),
            pltpu.VMEM((3, 2 * cells, cb), F32),
            pltpu.VMEM((ngx, cells, cb), BF16),
            pltpu.VMEM((ngx, cells, cb), BF16),
            dma((17,)),
            dma((8,)),
            dma((8,)),
            dma((ngx,)),
            dma((ngx,)),
            dma((ngx,)),
            dma((ngx,)),
            dma((ngx,)),
            dma((ngx,)),
            dma((ngx,)),
            dma((ngx,)),
            dma((ngx,)),
            dma((ngx,)),
        ],
        compiler_params=pltpu.CompilerParams(
            collective_id=0, has_side_effects=True, vmem_limit_bytes=52 << 20
        ),
    )
    arrays = (
        volume,
        fine_kernel,
        fine_bias.reshape(1, -1),
        down_kernel,
        down_bias.reshape(1, -1),
        bottle_kernel,
        bottle_bias.reshape(1, -1),
        up_kernel.reshape(ngx, cb, -1),
        up_bias.reshape(1, -1),
    )
    return call(*(pltpu.with_memory_space_constraint(a, pltpu.HBM) for a in arrays))


def solution(mesh):
    placed = (
        P(("groups", "gx"), ("gy", "col"), None),
        P(),
        P(),
        P(),
        P(),
        P(None, None, "gx"),
        P("gx"),
        P(),
        P(),
    )
    sizes = tuple(mesh.shape[name] for name in ("gx", "gy", "col"))
    return jax.shard_map(
        functools.partial(local, sizes),
        mesh=mesh,
        in_specs=placed,
        out_specs=P(("groups", "gx"), ("gy", "col"), None),
        check_vma=False,
    )
```

```python
import functools

import jax
import jax.numpy as jnp
from jax import lax
from jax.experimental import pallas as pl
from jax.experimental.pallas import tpu as pltpu
from jax.sharding import PartitionSpec as P

MESH = pl.DeviceIdType.MESH
F32 = jnp.float32
BF16 = jnp.bfloat16


def silu(a):
    return (0.5 * a) * (1.0 + jnp.tanh(0.5 * a))


def shifted(a, amount, depth):
    rows = a.shape[0]
    z = lax.broadcasted_iota(jnp.int32, a.shape, 0) % depth
    moved = pltpu.roll(a, amount % rows, 0)
    keep = z >= amount if amount > 0 else z < depth + amount
    return jnp.where(keep, moved, 0.0)


def body(
    sizes,
    vol_hbm,
    fk_hbm,
    fb_hbm,
    dk_hbm,
    db_hbm,
    bk_hbm,
    bb_hbm,
    uk_hbm,
    ub_hbm,
    out_ref,
    raw,
    brick,
    fk,
    band,
    dk,
    bk,
    uk,
    fb_ref,
    db_ref,
    bb_ref,
    ub_ref,
    fine_ref,
    strip,
    acc,
    sent,
    back,
    load_sem,
    halo_send,
    halo_recv,
    edge_send,
    edge_recv,
    rest_send,
    rest_recv,
    outer_send,
    outer_recv,
    inner_send,
    inner_recv,
    swap_send,
    swap_recv,
):
    ngx, ngy, ncol = sizes
    nq = ngy * ncol
    cx, cy, depth, pair = fine_ref.shape
    chans = pair // 2
    hx, hy = cx // 2, cy // 2
    cd = dk.shape[1]
    cb = bk.shape[2]
    g = lax.axis_index("gx")
    col = lax.axis_index("col")
    q = lax.axis_index("gy") * ncol + col

    def device(gg, qq):
        return {"gx": gg, "gy": qq // ncol, "col": qq % ncol}

    loads = [
        pltpu.make_async_copy(src, dst, load_sem.at[n])
        for n, (src, dst) in enumerate(
            (
                (vol_hbm, raw),
                (fk_hbm, fk),
                (fb_hbm, fb_ref),
                (dk_hbm, dk),
                (db_hbm, db_ref),
                (bb_hbm, bb_ref),
                (uk_hbm, uk),
                (ub_hbm, ub_ref),
            )
            + tuple((bk_hbm.at[pl.ds(3 * n, 3)], bk.at[pl.ds(3 * n, 3)]) for n in range(9))
        )
    ]
    for load in loads:
        load.start()

    brick[0] = jnp.zeros_like(brick[0])
    brick[cx + 1] = jnp.zeros_like(brick[0])
    for y in (0, cy + 1):
        brick[1 : cx + 1, y] = jnp.zeros((cx, depth, pair), BF16)
    strip[0] = jnp.zeros_like(strip[0])
    strip[ngx * hx + 1] = jnp.zeros_like(strip[0])

    @pl.when(q == 0)
    def _():
        strip[1 : ngx * hx + 1, 0] = jnp.zeros((ngx * hx, depth, cd), BF16)

    @pl.when(q == nq - 1)
    def _():
        strip[1 : ngx * hx + 1, hy + 1] = jnp.zeros((ngx * hx, depth, cd), BF16)

    def valid(gg, qq):
        ok = jnp.logical_and(gg >= 0, gg < ngx)
        return jnp.logical_and(ok, jnp.logical_and(qq >= 0, qq < nq))

    barrier = pltpu.get_barrier_semaphore()

    def greet(gg, qq):
        pl.semaphore_signal(barrier, inc=1, device_id=device(gg, qq), device_id_type=MESH)

    partners = ngx - 1
    for d in range(1, ngx):
        greet(lax.rem(g + d, ngx), q)
    for b in (-1, 1):
        there = valid(g, q + b)
        partners += jnp.where(there, ngx, 0)

        @pl.when(there)
        def _():
            for d in range(ngx):
                greet(lax.rem(g + d, ngx), q + b)

    loads[0].wait()
    for x in range(cx):
        brick[1 + x, 1 : cy + 1] = (
            raw[x].astype(F32).reshape(cy, depth, pair).astype(BF16)
        )
    pl.semaphore_wait(barrier, partners)

    def remote(src, dst, send, recv, gg, qq):
        return pltpu.make_async_remote_copy(
            src_ref=src,
            dst_ref=dst,
            send_sem=send,
            recv_sem=recv,
            device_id=device(gg, qq),
            device_id_type=MESH,
        )

    def edges(step, count):
        if step == 0:
            return pl.ds(1, count), pl.ds(1, count)
        if step > 0:
            return pl.ds(count, 1), pl.ds(0, 1)
        return pl.ds(1, 1), pl.ds(count + 1, 1)

    halos = []
    for a in (-1, 0, 1):
        for b in (-1, 0, 1):
            if a == 0 and b == 0:
                continue
            t = len(halos)
            sx, dx = edges(a, cx)
            sy, dy = edges(b, cy)
            halos.append(
                (
                    valid(g + a, q + b),
                    remote(
                        brick.at[sx, sy], brick.at[dx, dy],
                        halo_send.at[t], halo_recv.at[t], g + a, q + b,
                    ),
                    valid(g - a, q - b),
                    remote(
                        brick.at[dx, dy], brick.at[dx, dy],
                        halo_send.at[t], halo_recv.at[t], g - a, q - b,
                    ),
                )
            )
    for ok, out, _, _ in halos:
        pl.when(ok)(out.start)

    loads[1].wait()
    empty = jnp.zeros((chans, chans), BF16)
    for ij in range(9):
        f0, f1, f2 = fk[3 * ij], fk[3 * ij + 1], fk[3 * ij + 2]
        band[ij * pair : ij * pair + chans] = jnp.concatenate([f1, f0, empty, f2], axis=1)
        band[ij * pair + chans : (ij + 1) * pair] = jnp.concatenate([f2, f1, f0, empty], axis=1)

    for _, _, ok, into in halos:
        pl.when(ok)(into.wait_recv)

    pieces = [
        brick[i : i + cx, j : j + cy].reshape(cx * cy * depth, pair)
        for i in range(3)
        for j in range(3)
    ]
    loads[2].wait()
    prod = jnp.dot(jnp.concatenate(pieces, axis=1), band[...], preferred_element_type=F32)
    side = prod[:, pair:]
    lane = lax.broadcasted_iota(jnp.int32, side.shape, 1)
    fb = fb_ref[...]
    total = (
        prod[:, :pair]
        + jnp.where(lane < chans, shifted(side, 1, depth), shifted(side, -1, depth))
        + jnp.concatenate([fb, fb], axis=1)
    )
    fine_ref[...] = silu(total).astype(BF16).reshape(cx, cy, depth, pair)

    loads[3].wait()
    loads[4].wait()
    cells = []
    for x in range(hx):
        for y in range(hy):
            cells.append(
                jnp.concatenate(
                    [fine_ref[2 * x + dx, 2 * y + dy] for dx in (0, 1) for dy in (0, 1)], axis=1
                )
            )
    coarse = jnp.dot(jnp.concatenate(cells, axis=0), dk[...], preferred_element_type=F32)
    coarse = silu(coarse + db_ref[...]).astype(BF16)
    strip[pl.ds(1 + hx * g, hx), 1 : hy + 1] = coarse.reshape(hx, hy, depth, cd)

    def planes(at):
        return pl.ds(1 + hx * at, hx)

    inner = 1 - 2 * col
    inner_row = 1 + jnp.where(inner > 0, hy - 1, 0)
    outer_row = 1 + jnp.where(inner > 0, 0, hy - 1)
    inner_rim = jnp.where(inner > 0, 0, hy + 1)
    outer_rim = jnp.where(inner > 0, hy + 1, 0)
    mate = q + inner
    beyond = q - inner
    has_beyond = valid(g, beyond)
    first_row = jnp.where(has_beyond, outer_row, inner_row)
    rest_row = jnp.where(first_row == 1, 2, 1)

    def edge_block(source, to):
        ref = strip.at[planes(source), pl.ds(first_row, 1)]
        return remote(ref, ref, edge_send.at[to], edge_recv.at[source], to, q)

    def rest_block(source, to):
        ref = strip.at[planes(source), pl.ds(rest_row, hy - 1)]
        return remote(ref, ref, rest_send.at[to], rest_recv.at[source], to, q)

    def outer_out(source):
        return remote(
            strip.at[planes(source), pl.ds(outer_row, 1)], strip.at[planes(source), pl.ds(outer_rim, 1)],
            outer_send.at[source], outer_recv.at[source], g, beyond,
        )

    def outer_in(source):
        ref = strip.at[planes(source), pl.ds(inner_rim, 1)]
        return remote(ref, ref, outer_send.at[source], outer_recv.at[source], g, beyond)

    def inner_out(source):
        return remote(
            strip.at[planes(source), pl.ds(inner_row, 1)], strip.at[planes(source), pl.ds(inner_rim, 1)],
            inner_send.at[source], inner_recv.at[source], g, mate,
        )

    def inner_in(source):
        ref = strip.at[planes(source), pl.ds(outer_rim, 1)]
        return remote(ref, ref, inner_send.at[source], inner_recv.at[source], g, mate)

    def others(visit, order):
        for d in order:
            for p in (g + d, g - d):
                pl.when(valid(p, q))(functools.partial(visit, p))

    near = tuple(range(1, ngx))
    far = near[::-1]

    def spread(p):
        edge_block(g, p).start()
        rest_block(g, p).start()

    others(spread, far)
    pl.when(has_beyond)(outer_out(g).start)
    inner_out(g).start()
    for load in loads[5:]:
        load.wait()

    def forward(p):
        edge_block(p, p).wait_recv()
        pl.when(has_beyond)(outer_out(p).start)
        pl.when(jnp.logical_not(has_beyond))(inner_out(p).start)

    others(forward, far)

    def complete(p):
        rest_block(p, p).wait_recv()
        pl.when(has_beyond)(inner_out(p).start)

    others(complete, far)

    def swap(to, source):
        return remote(sent.at[to], back.at[source], swap_send.at[to], swap_recv.at[source], to, q)

    rows = hx * hy * depth

    def rims(p):
        inner_in(p).wait_recv()
        pl.when(has_beyond)(outer_in(p).wait_recv)

    @pl.loop(0, ngx - 1)
    def _(turn):
        n = ngx - 2 - turn
        step = jnp.where(n % 2 == 1, (n + 1) // 2, -((n + 1) // 2))
        at = g // 2 + step
        last = ngx // 2 - 1

        @pl.when(jnp.logical_and(at >= 0, at <= last))
        def _():
            low = jnp.where(step > 0, 2 * at - 1, jnp.where(at == 0, 2 * at, 2 * at + 1))
            high = jnp.where(step < 0, 2 * at + 2, jnp.where(at == last, 2 * at + 1, 2 * at))

            def arrivals(visit):
                for i in range(-1, 3):
                    p = 2 * at + i
                    new = jnp.logical_and(p >= low, p <= high)
                    pl.when(jnp.logical_and(new, valid(p, q)))(functools.partial(visit, p))

            def taps(j, k):
                return [
                    jnp.dot(
                        strip[pl.ds(2 * hx * at + i, 2 * hx), j : j + hy].reshape(2 * rows, cd),
                        bk[9 * i + 3 * j + k],
                        preferred_element_type=F32,
                    )
                    for i in range(3)
                ]

            for k in range(3):
                acc[k] = sum(taps(1, k))
            arrivals(rims)
            for k in range(3):
                acc[k] += sum(taps(0, k) + taps(2, k))
            bottle = acc[1] + shifted(acc[0], 1, depth) + shifted(acc[2], -1, depth)
            bottle = silu(bottle + bb_ref[...]).astype(BF16)
            for i in range(2):
                p = 2 * at + i
                sent[p] = bottle[i * rows : (i + 1) * rows]
                pl.when(p != g)(swap(p, g).start)

    lifted = jnp.dot(sent[g], uk[g], preferred_element_type=F32)
    for d in range(1, ngx):
        source = lax.rem(g + d, ngx)
        swap(source, source).wait_recv()
        lifted += jnp.dot(back[source], uk[source], preferred_element_type=F32)
    ub = ub_ref[...]
    ub = jnp.concatenate([ub, ub], axis=1)
    for x in range(hx):
        for dx in (0, 1):
            columns = []
            for y in range(hy):
                at = (x * hy + y) * depth
                for dy in (0, 1):
                    c = (2 * dx + dy) * pair
                    columns.append(
                        fine_ref[2 * x + dx, 2 * y + dy].astype(F32)
                        + (lifted[at : at + depth, c : c + pair] + ub)
                    )
            whole = jnp.stack(columns).reshape(cy, depth * pair)
            out_ref[2 * x + dx] = whole.astype(BF16)

    for ok, out, _, _ in halos:
        pl.when(ok)(out.wait_send)

    def left(p):
        edge_block(g, p).wait_send()
        rest_block(g, p).wait_send()
        swap(p, g).wait_send()

    others(left, near)
    for p in range(ngx):
        pl.when(has_beyond)(outer_out(p).wait_send)
        inner_out(p).wait_send()


def local(
    sizes,
    volume,
    fine_kernel,
    fine_bias,
    down_kernel,
    down_bias,
    bottle_kernel,
    bottle_bias,
    up_kernel,
    up_bias,
):
    ngx = sizes[0]
    cx, cy, merged = volume.shape
    chans = fine_kernel.shape[1]
    pair = 2 * chans
    depth = merged // pair
    hx, hy = cx // 2, cy // 2
    cd = down_kernel.shape[1]
    cb = bottle_kernel.shape[2]
    cells = hx * hy * depth
    hbm = pl.BlockSpec(memory_space=pltpu.HBM)
    vmem = pl.BlockSpec(memory_space=pltpu.VMEM)
    dma = pltpu.SemaphoreType.DMA
    call = pl.pallas_call(
        functools.partial(body, sizes),
        out_shape=jax.ShapeDtypeStruct((cx, cy, merged), BF16),
        in_specs=[hbm] * 9,
        out_specs=vmem,
        scratch_shapes=[
            pltpu.VMEM(volume.shape, BF16),
            pltpu.VMEM((cx + 2, cy + 2, depth, pair), BF16),
            pltpu.VMEM(fine_kernel.shape, BF16),
            pltpu.VMEM((9 * pair, 2 * pair), BF16),
            pltpu.VMEM(down_kernel.shape, BF16),
            pltpu.VMEM(bottle_kernel.shape, BF16),
            pltpu.VMEM((ngx, cb, up_kernel.shape[1]), BF16),
            pltpu.VMEM((1, chans), F32),
            pltpu.VMEM((1, cd), F32),
            pltpu.VMEM((1, cb), F32),
            pltpu.VMEM((1, chans), F32),
            pltpu.VMEM((cx, cy, depth, pair), BF16),
            pltpu.VMEM((ngx * hx + 2, hy + 2, depth, cd), BF16),
            pltpu.VMEM((3, 2 * cells, cb), F32),
            pltpu.VMEM((ngx, cells, cb), BF16),
            pltpu.VMEM((ngx, cells, cb), BF16),
            dma((17,)),
            dma((8,)),
            dma((8,)),
            dma((ngx,)),
            dma((ngx,)),
            dma((ngx,)),
            dma((ngx,)),
            dma((ngx,)),
            dma((ngx,)),
            dma((ngx,)),
            dma((ngx,)),
            dma((ngx,)),
            dma((ngx,)),
        ],
        compiler_params=pltpu.CompilerParams(
            collective_id=0, has_side_effects=True, vmem_limit_bytes=52 << 20
        ),
    )
    arrays = (
        volume,
        fine_kernel,
        fine_bias.reshape(1, -1),
        down_kernel,
        down_bias.reshape(1, -1),
        bottle_kernel,
        bottle_bias.reshape(1, -1),
        up_kernel.reshape(ngx, cb, -1),
        up_bias.reshape(1, -1),
    )
    return call(*(pltpu.with_memory_space_constraint(a, pltpu.HBM) for a in arrays))


def solution(mesh):
    placed = (
        P(("groups", "gx"), ("gy", "col"), None),
        P(),
        P(),
        P(),
        P(),
        P(None, None, "gx"),
        P("gx"),
        P(),
        P(),
    )
    sizes = tuple(mesh.shape[name] for name in ("gx", "gy", "col"))
    return jax.shard_map(
        functools.partial(local, sizes),
        mesh=mesh,
        in_specs=placed,
        out_specs=P(("groups", "gx"), ("gy", "col"), None),
        check_vma=False,
    )
```

```python
import functools

import jax
import jax.numpy as jnp
from jax import lax
from jax.experimental import pallas as pl
from jax.experimental.pallas import tpu as pltpu
from jax.sharding import PartitionSpec as P

MESH = pl.DeviceIdType.MESH
F32 = jnp.float32
BF16 = jnp.bfloat16


def silu(a):
    return (0.5 * a) * (1.0 + jnp.tanh(0.5 * a))


def shifted(a, amount, depth):
    rows = a.shape[0]
    z = lax.broadcasted_iota(jnp.int32, a.shape, 0) % depth
    moved = pltpu.roll(a, amount % rows, 0)
    keep = z >= amount if amount > 0 else z < depth + amount
    return jnp.where(keep, moved, 0.0)


def body(
    sizes,
    vol_hbm,
    fk_hbm,
    fb_hbm,
    dk_hbm,
    db_hbm,
    bk_hbm,
    bb_hbm,
    uk_hbm,
    ub_hbm,
    out_ref,
    raw,
    brick,
    fk,
    band,
    dk,
    bk,
    uk,
    fb_ref,
    db_ref,
    bb_ref,
    ub_ref,
    fine_ref,
    strip,
    acc,
    sent,
    back,
    word,
    load_sem,
    halo_send,
    halo_recv,
    edge_send,
    edge_recv,
    rest_send,
    rest_recv,
    outer_send,
    outer_recv,
    inner_send,
    inner_recv,
    swap_send,
    swap_recv,
):
    ngx, ngy, ncol = sizes
    nq = ngy * ncol
    cx, cy, depth, pair = fine_ref.shape
    chans = pair // 2
    hx, hy = cx // 2, cy // 2
    cd = dk.shape[1]
    cb = bk.shape[2]
    g = lax.axis_index("gx")
    col = lax.axis_index("col")
    q = lax.axis_index("gy") * ncol + col

    def device(gg, qq):
        return {"gx": gg, "gy": qq // ncol, "col": qq % ncol}

    loads = [
        pltpu.make_async_copy(src, dst, load_sem.at[n])
        for n, (src, dst) in enumerate(
            (
                (vol_hbm, raw),
                (fk_hbm, fk),
                (fb_hbm, fb_ref),
                (dk_hbm, dk),
                (db_hbm, db_ref),
                (bb_hbm, bb_ref),
                (uk_hbm, uk),
                (ub_hbm, ub_ref),
            )
            + tuple((bk_hbm.at[pl.ds(3 * n, 3)], bk.at[pl.ds(3 * n, 3)]) for n in range(9))
        )
    ]
    for load in loads:
        load.start()

    brick[0] = jnp.zeros_like(brick[0])
    brick[cx + 1] = jnp.zeros_like(brick[0])
    for y in (0, cy + 1):
        brick[1 : cx + 1, y] = jnp.zeros((cx, depth, pair), BF16)
    strip[0] = jnp.zeros_like(strip[0])
    strip[ngx * hx + 1] = jnp.zeros_like(strip[0])

    @pl.when(q == 0)
    def _():
        strip[1 : ngx * hx + 1, 0] = jnp.zeros((ngx * hx, depth, cd), BF16)

    @pl.when(q == nq - 1)
    def _():
        strip[1 : ngx * hx + 1, hy + 1] = jnp.zeros((ngx * hx, depth, cd), BF16)

    def valid(gg, qq):
        ok = jnp.logical_and(gg >= 0, gg < ngx)
        return jnp.logical_and(ok, jnp.logical_and(qq >= 0, qq < nq))

    barrier = pltpu.get_barrier_semaphore()

    def greet(gg, qq):
        pl.semaphore_signal(barrier, inc=1, device_id=device(gg, qq), device_id_type=MESH)

    partners = 0
    for a in (-1, 0, 1):
        for b in (-1, 0, 1):
            if a == 0 and b == 0:
                continue
            there = valid(g + a, q + b)
            pl.when(there)(functools.partial(greet, g + a, q + b))
            partners += there.astype(jnp.int32)

    loads[0].wait()
    for x in range(cx):
        brick[1 + x, 1 : cy + 1] = (
            raw[x].astype(F32).reshape(cy, depth, pair).astype(BF16)
        )
    pl.semaphore_wait(barrier, partners)

    def remote(src, dst, send, recv, gg, qq):
        return pltpu.make_async_remote_copy(
            src_ref=src,
            dst_ref=dst,
            send_sem=send,
            recv_sem=recv,
            device_id=device(gg, qq),
            device_id_type=MESH,
        )

    def edges(step, count):
        if step == 0:
            return pl.ds(1, count), pl.ds(1, count)
        if step > 0:
            return pl.ds(count, 1), pl.ds(0, 1)
        return pl.ds(1, 1), pl.ds(count + 1, 1)

    halos = []
    for a in (-1, 0, 1):
        for b in (-1, 0, 1):
            if a == 0 and b == 0:
                continue
            t = len(halos)
            sx, dx = edges(a, cx)
            sy, dy = edges(b, cy)
            halos.append(
                (
                    valid(g + a, q + b),
                    remote(
                        brick.at[sx, sy], brick.at[dx, dy],
                        halo_send.at[t], halo_recv.at[t], g + a, q + b,
                    ),
                    valid(g - a, q - b),
                    remote(
                        brick.at[dx, dy], brick.at[dx, dy],
                        halo_send.at[t], halo_recv.at[t], g - a, q - b,
                    ),
                )
            )
    for ok, out, _, _ in halos:
        pl.when(ok)(out.start)

    def tell(side):
        pl.semaphore_signal(
            word.at[side], inc=1, device_id=device(g + 2 * side - 1, q), device_id_type=MESH
        )

    between = jnp.logical_and(g > 0, g < ngx - 1)
    for side in (0, 1):
        pl.when(between)(functools.partial(tell, side))

    loads[1].wait()
    empty = jnp.zeros((chans, chans), BF16)
    for ij in range(9):
        f0, f1, f2 = fk[3 * ij], fk[3 * ij + 1], fk[3 * ij + 2]
        band[ij * pair : ij * pair + chans] = jnp.concatenate([f1, f0, empty, f2], axis=1)
        band[ij * pair + chans : (ij + 1) * pair] = jnp.concatenate([f2, f1, f0, empty], axis=1)

    for n in range(ngx - 2):
        for side in (0, 1):
            expected = ngx - 2 - g if side == 0 else g - 1

            @pl.when(n < expected)
            def _():
                pl.semaphore_wait(word.at[side], 1)
                pl.when(g > 0 if side == 0 else g < ngx - 1)(functools.partial(tell, side))

    for _, _, ok, into in halos:
        pl.when(ok)(into.wait_recv)

    pieces = [
        brick[i : i + cx, j : j + cy].reshape(cx * cy * depth, pair)
        for i in range(3)
        for j in range(3)
    ]
    loads[2].wait()
    prod = jnp.dot(jnp.concatenate(pieces, axis=1), band[...], preferred_element_type=F32)
    side = prod[:, pair:]
    lane = lax.broadcasted_iota(jnp.int32, side.shape, 1)
    fb = fb_ref[...]
    total = (
        prod[:, :pair]
        + jnp.where(lane < chans, shifted(side, 1, depth), shifted(side, -1, depth))
        + jnp.concatenate([fb, fb], axis=1)
    )
    fine_ref[...] = silu(total).astype(BF16).reshape(cx, cy, depth, pair)

    loads[3].wait()
    loads[4].wait()
    cells = []
    for x in range(hx):
        for y in range(hy):
            cells.append(
                jnp.concatenate(
                    [fine_ref[2 * x + dx, 2 * y + dy] for dx in (0, 1) for dy in (0, 1)], axis=1
                )
            )
    coarse = jnp.dot(jnp.concatenate(cells, axis=0), dk[...], preferred_element_type=F32)
    coarse = silu(coarse + db_ref[...]).astype(BF16)
    strip[pl.ds(1 + hx * g, hx), 1 : hy + 1] = coarse.reshape(hx, hy, depth, cd)

    def planes(at):
        return pl.ds(1 + hx * at, hx)

    inner = 1 - 2 * col
    inner_row = 1 + jnp.where(inner > 0, hy - 1, 0)
    outer_row = 1 + jnp.where(inner > 0, 0, hy - 1)
    inner_rim = jnp.where(inner > 0, 0, hy + 1)
    outer_rim = jnp.where(inner > 0, hy + 1, 0)
    mate = q + inner
    beyond = q - inner
    has_beyond = valid(g, beyond)
    first_row = jnp.where(has_beyond, outer_row, inner_row)
    rest_row = jnp.where(first_row == 1, 2, 1)

    def edge_block(source, to):
        ref = strip.at[planes(source), pl.ds(first_row, 1)]
        return remote(ref, ref, edge_send.at[to], edge_recv.at[source], to, q)

    def rest_block(source, to):
        ref = strip.at[planes(source), pl.ds(rest_row, hy - 1)]
        return remote(ref, ref, rest_send.at[to], rest_recv.at[source], to, q)

    def outer_out(source):
        return remote(
            strip.at[planes(source), pl.ds(outer_row, 1)], strip.at[planes(source), pl.ds(outer_rim, 1)],
            outer_send.at[source], outer_recv.at[source], g, beyond,
        )

    def outer_in(source):
        ref = strip.at[planes(source), pl.ds(inner_rim, 1)]
        return remote(ref, ref, outer_send.at[source], outer_recv.at[source], g, beyond)

    def inner_out(source):
        return remote(
            strip.at[planes(source), pl.ds(inner_row, 1)], strip.at[planes(source), pl.ds(inner_rim, 1)],
            inner_send.at[source], inner_recv.at[source], g, mate,
        )

    def inner_in(source):
        ref = strip.at[planes(source), pl.ds(outer_rim, 1)]
        return remote(ref, ref, inner_send.at[source], inner_recv.at[source], g, mate)

    def others(visit, order):
        for d in order:
            for p in (g + d, g - d):
                pl.when(valid(p, q))(functools.partial(visit, p))

    near = tuple(range(1, ngx))
    far = near[::-1]

    def spread(p):
        edge_block(g, p).start()
        rest_block(g, p).start()

    others(spread, far)
    pl.when(has_beyond)(outer_out(g).start)
    inner_out(g).start()
    for load in loads[5:]:
        load.wait()

    def forward(p):
        edge_block(p, p).wait_recv()
        pl.when(has_beyond)(outer_out(p).start)
        pl.when(jnp.logical_not(has_beyond))(inner_out(p).start)

    others(forward, far)

    def complete(p):
        rest_block(p, p).wait_recv()
        pl.when(has_beyond)(inner_out(p).start)

    others(complete, far)

    def swap(to, source):
        return remote(sent.at[to], back.at[source], swap_send.at[to], swap_recv.at[source], to, q)

    rows = hx * hy * depth

    def rims(p):
        inner_in(p).wait_recv()
        pl.when(has_beyond)(outer_in(p).wait_recv)

    @pl.loop(0, ngx - 1)
    def _(turn):
        n = ngx - 2 - turn
        step = jnp.where(n % 2 == 1, (n + 1) // 2, -((n + 1) // 2))
        at = g // 2 + step
        last = ngx // 2 - 1

        @pl.when(jnp.logical_and(at >= 0, at <= last))
        def _():
            low = jnp.where(step > 0, 2 * at - 1, jnp.where(at == 0, 2 * at, 2 * at + 1))
            high = jnp.where(step < 0, 2 * at + 2, jnp.where(at == last, 2 * at + 1, 2 * at))

            def arrivals(visit):
                for i in range(-1, 3):
                    p = 2 * at + i
                    new = jnp.logical_and(p >= low, p <= high)
                    pl.when(jnp.logical_and(new, valid(p, q)))(functools.partial(visit, p))

            def taps(j, k):
                return [
                    jnp.dot(
                        strip[pl.ds(2 * hx * at + i, 2 * hx), j : j + hy].reshape(2 * rows, cd),
                        bk[9 * i + 3 * j + k],
                        preferred_element_type=F32,
                    )
                    for i in range(3)
                ]

            for k in range(3):
                acc[k] = sum(taps(1, k))
            arrivals(rims)
            for k in range(3):
                acc[k] += sum(taps(0, k) + taps(2, k))
            bottle = acc[1] + shifted(acc[0], 1, depth) + shifted(acc[2], -1, depth)
            bottle = silu(bottle + bb_ref[...]).astype(BF16)
            for i in range(2):
                p = 2 * at + i
                sent[p] = bottle[i * rows : (i + 1) * rows]
                pl.when(p != g)(swap(p, g).start)

    lifted = jnp.dot(sent[g], uk[g], preferred_element_type=F32)
    for d in range(1, ngx):
        source = lax.rem(g + d, ngx)
        swap(source, source).wait_recv()
        lifted += jnp.dot(back[source], uk[source], preferred_element_type=F32)
    ub = ub_ref[...]
    ub = jnp.concatenate([ub, ub], axis=1)
    for x in range(hx):
        for dx in (0, 1):
            columns = []
            for y in range(hy):
                at = (x * hy + y) * depth
                for dy in (0, 1):
                    c = (2 * dx + dy) * pair
                    columns.append(
                        fine_ref[2 * x + dx, 2 * y + dy].astype(F32)
                        + (lifted[at : at + depth, c : c + pair] + ub)
                    )
            whole = jnp.stack(columns).reshape(cy, depth * pair)
            out_ref[2 * x + dx] = whole.astype(BF16)

    for ok, out, _, _ in halos:
        pl.when(ok)(out.wait_send)

    def left(p):
        edge_block(g, p).wait_send()
        rest_block(g, p).wait_send()
        swap(p, g).wait_send()

    others(left, near)
    for p in range(ngx):
        pl.when(has_beyond)(outer_out(p).wait_send)
        inner_out(p).wait_send()


def local(
    sizes,
    volume,
    fine_kernel,
    fine_bias,
    down_kernel,
    down_bias,
    bottle_kernel,
    bottle_bias,
    up_kernel,
    up_bias,
):
    ngx = sizes[0]
    cx, cy, merged = volume.shape
    chans = fine_kernel.shape[1]
    pair = 2 * chans
    depth = merged // pair
    hx, hy = cx // 2, cy // 2
    cd = down_kernel.shape[1]
    cb = bottle_kernel.shape[2]
    cells = hx * hy * depth
    hbm = pl.BlockSpec(memory_space=pltpu.HBM)
    vmem = pl.BlockSpec(memory_space=pltpu.VMEM)
    dma = pltpu.SemaphoreType.DMA
    call = pl.pallas_call(
        functools.partial(body, sizes),
        out_shape=jax.ShapeDtypeStruct((cx, cy, merged), BF16),
        in_specs=[hbm] * 9,
        out_specs=vmem,
        scratch_shapes=[
            pltpu.VMEM(volume.shape, BF16),
            pltpu.VMEM((cx + 2, cy + 2, depth, pair), BF16),
            pltpu.VMEM(fine_kernel.shape, BF16),
            pltpu.VMEM((9 * pair, 2 * pair), BF16),
            pltpu.VMEM(down_kernel.shape, BF16),
            pltpu.VMEM(bottle_kernel.shape, BF16),
            pltpu.VMEM((ngx, cb, up_kernel.shape[1]), BF16),
            pltpu.VMEM((1, chans), F32),
            pltpu.VMEM((1, cd), F32),
            pltpu.VMEM((1, cb), F32),
            pltpu.VMEM((1, chans), F32),
            pltpu.VMEM((cx, cy, depth, pair), BF16),
            pltpu.VMEM((ngx * hx + 2, hy + 2, depth, cd), BF16),
            pltpu.VMEM((3, 2 * cells, cb), F32),
            pltpu.VMEM((ngx, cells, cb), BF16),
            pltpu.VMEM((ngx, cells, cb), BF16),
            pltpu.SemaphoreType.REGULAR((2,)),
            dma((17,)),
            dma((8,)),
            dma((8,)),
            dma((ngx,)),
            dma((ngx,)),
            dma((ngx,)),
            dma((ngx,)),
            dma((ngx,)),
            dma((ngx,)),
            dma((ngx,)),
            dma((ngx,)),
            dma((ngx,)),
            dma((ngx,)),
        ],
        compiler_params=pltpu.CompilerParams(
            collective_id=0, has_side_effects=True, vmem_limit_bytes=52 << 20
        ),
    )
    arrays = (
        volume,
        fine_kernel,
        fine_bias.reshape(1, -1),
        down_kernel,
        down_bias.reshape(1, -1),
        bottle_kernel,
        bottle_bias.reshape(1, -1),
        up_kernel.reshape(ngx, cb, -1),
        up_bias.reshape(1, -1),
    )
    return call(*(pltpu.with_memory_space_constraint(a, pltpu.HBM) for a in arrays))


def solution(mesh):
    placed = (
        P(("groups", "gx"), ("gy", "col"), None),
        P(),
        P(),
        P(),
        P(),
        P(None, None, "gx"),
        P("gx"),
        P(),
        P(),
    )
    sizes = tuple(mesh.shape[name] for name in ("gx", "gy", "col"))
    return jax.shard_map(
        functools.partial(local, sizes),
        mesh=mesh,
        in_specs=placed,
        out_specs=P(("groups", "gx"), ("gy", "col"), None),
        check_vma=False,
    )
```

```python
import functools

import jax
import jax.numpy as jnp
from jax import lax
from jax.experimental import pallas as pl
from jax.experimental.pallas import tpu as pltpu
from jax.sharding import PartitionSpec as P

MESH = pl.DeviceIdType.MESH
F32 = jnp.float32
BF16 = jnp.bfloat16


def silu(a):
    return (0.5 * a) * (1.0 + jnp.tanh(0.5 * a))


def shifted(a, amount, depth):
    rows = a.shape[0]
    z = lax.broadcasted_iota(jnp.int32, a.shape, 0) % depth
    moved = pltpu.roll(a, amount % rows, 0)
    keep = z >= amount if amount > 0 else z < depth + amount
    return jnp.where(keep, moved, 0.0)


def body(
    sizes,
    vol_hbm,
    fk_hbm,
    fb_hbm,
    dk_hbm,
    db_hbm,
    bk_hbm,
    bb_hbm,
    uk_hbm,
    ub_hbm,
    out_ref,
    raw,
    brick,
    fk,
    band,
    dk,
    bk,
    uk,
    fb_ref,
    db_ref,
    bb_ref,
    ub_ref,
    fine_ref,
    strip,
    acc,
    sent,
    back,
    load_sem,
    block_send,
    block_recv,
    outer_send,
    outer_recv,
    inner_send,
    inner_recv,
    swap_send,
    swap_recv,
):
    ngx, ngy, ncol = sizes
    nq = ngy * ncol
    cx, wide, depth, pair = fine_ref.shape
    cy = wide - 4
    chans = pair // 2
    hx, hy = cx // 2, cy // 2
    cd = dk.shape[1]
    cb = bk.shape[2]
    g = lax.axis_index("gx")
    col = lax.axis_index("col")
    q = lax.axis_index("gy") * ncol + col

    def device(gg, qq):
        return {"gx": gg, "gy": qq // ncol, "col": qq % ncol}

    loads = [
        pltpu.make_async_copy(src, dst, load_sem.at[n])
        for n, (src, dst) in enumerate(
            (
                (vol_hbm, raw),
                (fk_hbm, fk),
                (fb_hbm, fb_ref),
                (dk_hbm, dk),
                (db_hbm, db_ref),
                (bb_hbm, bb_ref),
                (uk_hbm, uk),
                (ub_hbm, ub_ref),
            )
            + tuple((bk_hbm.at[pl.ds(3 * n, 3)], bk.at[pl.ds(3 * n, 3)]) for n in range(9))
        )
    ]
    for load in loads:
        load.start()

    rim = 3
    half = cy // 2 + 2
    brick[0] = jnp.zeros_like(brick[0])
    brick[ngx * cx + 1] = jnp.zeros_like(brick[0])
    strip[0] = jnp.zeros_like(strip[0])
    strip[ngx * hx + 1] = jnp.zeros_like(strip[0])

    @pl.when(q == 0)
    def _():
        brick[1 : ngx * cx + 1, :rim] = jnp.zeros((ngx * cx, rim, depth, pair), BF16)

    @pl.when(q == nq - 1)
    def _():
        brick[1 : ngx * cx + 1, rim + cy :] = jnp.zeros((ngx * cx, rim, depth, pair), BF16)

    def valid(gg, qq):
        ok = jnp.logical_and(gg >= 0, gg < ngx)
        return jnp.logical_and(ok, jnp.logical_and(qq >= 0, qq < nq))

    barrier = pltpu.get_barrier_semaphore()

    def greet(gg, qq):
        pl.semaphore_signal(barrier, inc=1, device_id=device(gg, qq), device_id_type=MESH)

    inner = 1 - 2 * col
    mate = q + inner
    beyond = q - inner
    has_beyond = valid(g, beyond)
    for d in range(1, ngx):
        greet(lax.rem(g + d, ngx), q)
    greet(g, mate)
    pl.when(has_beyond)(functools.partial(greet, g, beyond))

    loads[0].wait()
    for x in range(cx):
        brick[1 + cx * g + x, rim : rim + cy] = (
            raw[x].astype(F32).reshape(cy, depth, pair).astype(BF16)
        )
    pl.semaphore_wait(barrier, ngx + has_beyond.astype(jnp.int32))

    def remote(src, dst, send, recv, gg, qq):
        return pltpu.make_async_remote_copy(
            src_ref=src,
            dst_ref=dst,
            send_sem=send,
            recv_sem=recv,
            device_id=device(gg, qq),
            device_id_type=MESH,
        )

    def layers(at):
        return pl.ds(1 + cx * at, cx)

    def block(source, to):
        ref = brick.at[layers(source), pl.ds(rim, cy)]
        return remote(ref, ref, block_send.at[to], block_recv.at[source], to, q)

    def rows_out(at, b, send, recv, beside):
        src = jnp.where(b > 0, cy, rim)
        dst = jnp.where(b > 0, 0, rim + cy)
        return remote(
            brick.at[layers(at), pl.ds(src, rim)], brick.at[layers(at), pl.ds(dst, rim)],
            send.at[at], recv.at[at], g, beside,
        )

    def rows_in(at, b, send, recv, beside):
        ref = brick.at[layers(at), pl.ds(jnp.where(b > 0, rim + cy, 0), rim)]
        return remote(ref, ref, send.at[at], recv.at[at], g, beside)

    def inner_out(at):
        return rows_out(at, inner, inner_send, inner_recv, mate)

    def inner_in(at):
        return rows_in(at, inner, inner_send, inner_recv, mate)

    def outer_out(at):
        return rows_out(at, -inner, outer_send, outer_recv, beyond)

    def outer_in(at):
        return rows_in(at, -inner, outer_send, outer_recv, beyond)

    def others(visit, order):
        for d in order:
            for p in (g + d, g - d):
                pl.when(valid(p, q))(functools.partial(visit, p))

    near = tuple(range(1, ngx))
    far = near[::-1]

    def forward(p):
        pl.when(has_beyond)(outer_out(p).start)
        inner_out(p).start()

    others(lambda p: block(g, p).start(), far)
    forward(g)

    loads[1].wait()
    empty = jnp.zeros((chans, chans), BF16)
    for ij in range(9):
        f0, f1, f2 = fk[3 * ij], fk[3 * ij + 1], fk[3 * ij + 2]
        band[ij * pair : ij * pair + chans] = jnp.concatenate([f1, f0, empty, f2], axis=1)
        band[ij * pair + chans : (ij + 1) * pair] = jnp.concatenate([f2, f1, f0, empty], axis=1)

    def arrive(p):
        block(p, p).wait_recv()
        forward(p)

    others(arrive, far)
    for load in loads[2:5]:
        load.wait()
    for p in range(ngx):
        inner_in(p).wait_recv()

    @pl.loop(0, ngx)
    def _(unit):
        side, at = unit // (ngx // 2), unit % (ngx // 2)

        @pl.when(jnp.logical_and(unit == ngx // 2, has_beyond))
        def _():
            for p in range(ngx):
                outer_in(p).wait_recv()

        top = jnp.where((side == 0) == (inner > 0), half, 0)
        pieces = [
            brick[pl.ds(2 * cx * at + i, 2 * cx), pl.ds(top + j, half)].reshape(2 * cx * half * depth, pair)
            for i in range(3)
            for j in range(3)
        ]
        prod = jnp.dot(jnp.concatenate(pieces, axis=1), band[...], preferred_element_type=F32)
        wing = prod[:, pair:]
        lane = lax.broadcasted_iota(jnp.int32, wing.shape, 1)
        fb = fb_ref[...]
        total = (
            prod[:, :pair]
            + jnp.where(lane < chans, shifted(wing, 1, depth), shifted(wing, -1, depth))
            + jnp.concatenate([fb, fb], axis=1)
        )
        fine = silu(total).astype(BF16).reshape(2 * cx, half, depth, pair)
        for i in range(2):

            @pl.when(2 * at + i == g)
            def _():
                fine_ref[:, pl.ds(top, half)] = fine[i * cx : (i + 1) * cx]

        cells = [
            jnp.concatenate(
                [fine[2 * x + dx, 2 * y + dy] for dx in (0, 1) for dy in (0, 1)], axis=1
            )
            for x in range(2 * hx)
            for y in range(half // 2)
        ]
        coarse = jnp.dot(jnp.concatenate(cells, axis=0), dk[...], preferred_element_type=F32)
        coarse = silu(coarse + db_ref[...]).astype(BF16).reshape(2 * hx, half // 2, depth, cd)
        strip[pl.ds(1 + 2 * hx * at, 2 * hx), pl.ds(top // 2, half // 2)] = coarse

        @pl.when(jnp.logical_and(q == 0, top == 0))
        def _():
            strip[pl.ds(1 + 2 * hx * at, 2 * hx), 0] = jnp.zeros((2 * hx, depth, cd), BF16)

        @pl.when(jnp.logical_and(q == nq - 1, top > 0))
        def _():
            strip[pl.ds(1 + 2 * hx * at, 2 * hx), hy + 1] = jnp.zeros((2 * hx, depth, cd), BF16)

    for load in loads[5:]:
        load.wait()

    def swap(to, source):
        return remote(sent.at[to], back.at[source], swap_send.at[to], swap_recv.at[source], to, q)

    rows = hx * hy * depth

    @pl.loop(0, ngx - 1)
    def _(turn):
        n = ngx - 2 - turn
        step = jnp.where(n % 2 == 1, (n + 1) // 2, -((n + 1) // 2))
        at = g // 2 + step
        last = ngx // 2 - 1

        @pl.when(jnp.logical_and(at >= 0, at <= last))
        def _():
            def taps(j, k):
                return [
                    jnp.dot(
                        strip[pl.ds(2 * hx * at + i, 2 * hx), j : j + hy].reshape(2 * rows, cd),
                        bk[9 * i + 3 * j + k],
                        preferred_element_type=F32,
                    )
                    for i in range(3)
                ]

            for k in range(3):
                acc[k] = sum(taps(0, k) + taps(1, k) + taps(2, k))
            bottle = acc[1] + shifted(acc[0], 1, depth) + shifted(acc[2], -1, depth)
            bottle = silu(bottle + bb_ref[...]).astype(BF16)
            for i in range(2):
                p = 2 * at + i
                sent[p] = bottle[i * rows : (i + 1) * rows]
                pl.when(p != g)(swap(p, g).start)

    lifted = jnp.dot(sent[g], uk[g], preferred_element_type=F32)
    for d in range(1, ngx):
        source = lax.rem(g + d, ngx)
        swap(source, source).wait_recv()
        lifted += jnp.dot(back[source], uk[source], preferred_element_type=F32)
    ub = ub_ref[...]
    ub = jnp.concatenate([ub, ub], axis=1)
    for x in range(hx):
        for dx in (0, 1):
            columns = []
            for y in range(hy):
                at = (x * hy + y) * depth
                for dy in (0, 1):
                    c = (2 * dx + dy) * pair
                    columns.append(
                        fine_ref[2 * x + dx, 2 + 2 * y + dy].astype(F32)
                        + (lifted[at : at + depth, c : c + pair] + ub)
                    )
            whole = jnp.stack(columns).reshape(cy, depth * pair)
            out_ref[2 * x + dx] = whole.astype(BF16)

    def left(p):
        block(g, p).wait_send()
        swap(p, g).wait_send()

    others(left, near)
    for p in range(ngx):
        pl.when(has_beyond)(outer_out(p).wait_send)
        inner_out(p).wait_send()


def local(
    sizes,
    volume,
    fine_kernel,
    fine_bias,
    down_kernel,
    down_bias,
    bottle_kernel,
    bottle_bias,
    up_kernel,
    up_bias,
):
    ngx = sizes[0]
    cx, cy, merged = volume.shape
    chans = fine_kernel.shape[1]
    pair = 2 * chans
    depth = merged // pair
    hx, hy = cx // 2, cy // 2
    cd = down_kernel.shape[1]
    cb = bottle_kernel.shape[2]
    cells = hx * hy * depth
    hbm = pl.BlockSpec(memory_space=pltpu.HBM)
    vmem = pl.BlockSpec(memory_space=pltpu.VMEM)
    dma = pltpu.SemaphoreType.DMA
    call = pl.pallas_call(
        functools.partial(body, sizes),
        out_shape=jax.ShapeDtypeStruct((cx, cy, merged), BF16),
        in_specs=[hbm] * 9,
        out_specs=vmem,
        scratch_shapes=[
            pltpu.VMEM(volume.shape, BF16),
            pltpu.VMEM((ngx * cx + 2, cy + 6, depth, pair), BF16),
            pltpu.VMEM(fine_kernel.shape, BF16),
            pltpu.VMEM((9 * pair, 2 * pair), BF16),
            pltpu.VMEM(down_kernel.shape, BF16),
            pltpu.VMEM(bottle_kernel.shape, BF16),
            pltpu.VMEM((ngx, cb, up_kernel.shape[1]), BF16),
            pltpu.VMEM((1, chans), F32),
            pltpu.VMEM((1, cd), F32),
            pltpu.VMEM((1, cb), F32),
            pltpu.VMEM((1, chans), F32),
            pltpu.VMEM((cx, cy + 4, depth, pair), BF16),
            pltpu.VMEM((ngx * hx + 2, hy + 2, depth, cd), BF16),
            pltpu.VMEM((3, 2 * cells, cb), F32),
            pltpu.VMEM((ngx, cells, cb), BF16),
            pltpu.VMEM((ngx, cells, cb), BF16),
            dma((17,)),
            dma((ngx,)),
            dma((ngx,)),
            dma((ngx,)),
            dma((ngx,)),
            dma((ngx,)),
            dma((ngx,)),
            dma((ngx,)),
            dma((ngx,)),
        ],
        compiler_params=pltpu.CompilerParams(
            collective_id=0, has_side_effects=True, vmem_limit_bytes=52 << 20
        ),
    )
    arrays = (
        volume,
        fine_kernel,
        fine_bias.reshape(1, -1),
        down_kernel,
        down_bias.reshape(1, -1),
        bottle_kernel,
        bottle_bias.reshape(1, -1),
        up_kernel.reshape(ngx, cb, -1),
        up_bias.reshape(1, -1),
    )
    return call(*(pltpu.with_memory_space_constraint(a, pltpu.HBM) for a in arrays))


def solution(mesh):
    placed = (
        P(("groups", "gx"), ("gy", "col"), None),
        P(),
        P(),
        P(),
        P(),
        P(None, None, "gx"),
        P("gx"),
        P(),
        P(),
    )
    sizes = tuple(mesh.shape[name] for name in ("gx", "gy", "col"))
    return jax.shard_map(
        functools.partial(local, sizes),
        mesh=mesh,
        in_specs=placed,
        out_specs=P(("groups", "gx"), ("gy", "col"), None),
        check_vma=False,
    )
```

```python
import functools

import jax
import jax.numpy as jnp
from jax import lax
from jax.experimental import pallas as pl
from jax.experimental.pallas import tpu as pltpu
from jax.sharding import PartitionSpec as P

MESH = pl.DeviceIdType.MESH
F32 = jnp.float32
BF16 = jnp.bfloat16
FINE_PLANES = 2


def silu(a):
    return (0.5 * a) * (1.0 + jnp.tanh(0.5 * a))


def shifted(a, amount, depth):
    rows = a.shape[0]
    z = lax.broadcasted_iota(jnp.int32, a.shape, 0) % depth
    moved = pltpu.roll(a, amount % rows, 0)
    keep = z >= amount if amount > 0 else z < depth + amount
    return jnp.where(keep, moved, 0.0)


def body(
    sizes,
    vol_hbm,
    fk_hbm,
    fb_hbm,
    dk_hbm,
    db_hbm,
    bk_hbm,
    bb_hbm,
    uk_hbm,
    ub_hbm,
    out_ref,
    raw,
    brick,
    fk,
    band,
    dk,
    bk,
    uk,
    fb_ref,
    db_ref,
    bb_ref,
    ub_ref,
    fine_ref,
    strip,
    acc,
    sent,
    back,
    load_sem,
    block_send,
    block_recv,
    outer_send,
    outer_recv,
    inner_send,
    inner_recv,
    swap_send,
    swap_recv,
    share_send,
    share_recv,
):
    ngx, ngy, ncol = sizes
    nq = ngy * ncol
    cx, cy = raw.shape[:2]
    depth, pair = fine_ref.shape[2:]
    chans = pair // 2
    hx, hy = cx // 2, cy // 2
    cd = dk.shape[1]
    cb = bk.shape[2]
    g = lax.axis_index("gx")
    col = lax.axis_index("col")
    q = lax.axis_index("gy") * ncol + col

    def device(gg, qq):
        return {"gx": gg, "gy": qq // ncol, "col": qq % ncol}

    loads = [
        pltpu.make_async_copy(src, dst, load_sem.at[n])
        for n, (src, dst) in enumerate(
            (
                (vol_hbm, raw),
                (fk_hbm, fk),
                (fb_hbm, fb_ref),
                (dk_hbm, dk),
                (db_hbm, db_ref),
                (bb_hbm, bb_ref),
                (uk_hbm, uk),
                (ub_hbm, ub_ref),
            )
            + tuple((bk_hbm.at[pl.ds(3 * n, 3)], bk.at[pl.ds(3 * n, 3)]) for n in range(9))
        )
    ]
    for load in loads:
        load.start()

    rim = 3
    half = cy // 2 + 2
    brick[0] = jnp.zeros_like(brick[0])
    brick[ngx * cx + 1] = jnp.zeros_like(brick[0])
    strip[0] = jnp.zeros_like(strip[0])
    strip[ngx * hx + 1] = jnp.zeros_like(strip[0])

    @pl.when(q == 0)
    def _():
        brick[1 : ngx * cx + 1, :rim] = jnp.zeros((ngx * cx, rim, depth, pair), BF16)

    @pl.when(q == nq - 1)
    def _():
        brick[1 : ngx * cx + 1, rim + cy :] = jnp.zeros((ngx * cx, rim, depth, pair), BF16)

    def valid(gg, qq):
        ok = jnp.logical_and(gg >= 0, gg < ngx)
        return jnp.logical_and(ok, jnp.logical_and(qq >= 0, qq < nq))

    barrier = pltpu.get_barrier_semaphore()

    def greet(gg, qq):
        pl.semaphore_signal(barrier, inc=1, device_id=device(gg, qq), device_id_type=MESH)

    inner = 1 - 2 * col
    mate = q + inner
    beyond = q - inner
    has_beyond = valid(g, beyond)
    for d in range(1, ngx):
        greet(lax.rem(g + d, ngx), q)
    greet(g, mate)
    pl.when(has_beyond)(functools.partial(greet, g, beyond))

    loads[0].wait()
    for x in range(cx):
        brick[1 + cx * g + x, rim : rim + cy] = (
            raw[x].astype(F32).reshape(cy, depth, pair).astype(BF16)
        )
    pl.semaphore_wait(barrier, ngx + has_beyond.astype(jnp.int32))

    def remote(src, dst, send, recv, gg, qq):
        return pltpu.make_async_remote_copy(
            src_ref=src,
            dst_ref=dst,
            send_sem=send,
            recv_sem=recv,
            device_id=device(gg, qq),
            device_id_type=MESH,
        )

    def layers(at):
        return pl.ds(1 + cx * at, cx)

    def block(source, to):
        ref = brick.at[layers(source), pl.ds(rim, cy)]
        return remote(ref, ref, block_send.at[to], block_recv.at[source], to, q)

    def rows_out(at, b, count, send, recv, beside):
        src = jnp.where(b > 0, rim + cy - count, rim)
        dst = jnp.where(b > 0, rim - count, rim + cy)
        return remote(
            brick.at[layers(at), pl.ds(src, count)], brick.at[layers(at), pl.ds(dst, count)],
            send.at[at], recv.at[at], g, beside,
        )

    def rows_in(at, b, count, send, recv, beside):
        ref = brick.at[layers(at), pl.ds(jnp.where(b > 0, rim + cy, rim - count), count)]
        return remote(ref, ref, send.at[at], recv.at[at], g, beside)

    def inner_out(at):
        return rows_out(at, inner, 1, inner_send, inner_recv, mate)

    def inner_in(at):
        return rows_in(at, inner, 1, inner_send, inner_recv, mate)

    def outer_out(at):
        return rows_out(at, -inner, rim, outer_send, outer_recv, beyond)

    def outer_in(at):
        return rows_in(at, -inner, rim, outer_send, outer_recv, beyond)

    def others(visit, order):
        for d in order:
            for p in (g + d, g - d):
                pl.when(valid(p, q))(functools.partial(visit, p))

    near = tuple(range(1, ngx))
    far = near[::-1]

    def forward(p):
        pl.when(has_beyond)(outer_out(p).start)
        inner_out(p).start()

    others(lambda p: block(g, p).start(), far)
    forward(g)

    loads[1].wait()
    empty = jnp.zeros((chans, chans), BF16)
    for ij in range(9):
        f0, f1, f2 = fk[3 * ij], fk[3 * ij + 1], fk[3 * ij + 2]
        band[ij * pair : ij * pair + chans] = jnp.concatenate([f1, f0, empty, f2], axis=1)
        band[ij * pair + chans : (ij + 1) * pair] = jnp.concatenate([f2, f1, f0, empty], axis=1)

    def arrive(p):
        block(p, p).wait_recv()
        forward(p)

    others(arrive, far)
    for load in loads[2:5]:
        load.wait()
    for p in range(ngx):
        inner_in(p).wait_recv()

    group = FINE_PLANES
    bunch = min(ngx, 4)

    def fine_rows(top, count):
        @pl.loop(0, ngx // group)
        def _(n):
            layer = group * cx * n
            pieces = [
                brick[pl.ds(layer + i, group * cx), pl.ds(top + j, count)].reshape(group * cx * count * depth, pair)
                for i in range(3)
                for j in range(3)
            ]
            prod = jnp.dot(jnp.concatenate(pieces, axis=1), band[...], preferred_element_type=F32)
            wing = prod[:, pair:]
            lane = lax.broadcasted_iota(jnp.int32, wing.shape, 1)
            fb = fb_ref[...]
            total = (
                prod[:, :pair]
                + jnp.where(lane < chans, shifted(wing, 1, depth), shifted(wing, -1, depth))
                + jnp.concatenate([fb, fb], axis=1)
            )
            fine = silu(total).astype(BF16).reshape(group * cx, count, depth, pair)
            fine_ref[pl.ds(layer, group * cx), pl.ds(top, count)] = fine

    def coarse_rows(top, count):
        @pl.loop(0, ngx // bunch)
        def _(n):
            fine = fine_ref[pl.ds(bunch * cx * n, bunch * cx), pl.ds(top, 2 * count)]
            cells = [
                jnp.concatenate(
                    [fine[2 * x + dx, 2 * y + dy] for dx in (0, 1) for dy in (0, 1)], axis=1
                )
                for x in range(bunch * hx)
                for y in range(count)
            ]
            coarse = jnp.dot(jnp.concatenate(cells, axis=0), dk[...], preferred_element_type=F32)
            coarse = silu(coarse + db_ref[...]).astype(BF16)
            strip[pl.ds(1 + bunch * hx * n, bunch * hx), pl.ds(top // 2, count)] = coarse.reshape(
                bunch * hx, count, depth, cd
            )

    early = jnp.where(inner > 0, 3, 2)
    late = jnp.where(inner > 0, 0, cy + 1)
    fine_rows(early, cy - 1)
    coarse_rows(jnp.where(inner > 0, 4, 2), hy - 1)

    def share(sending):
        mine = jnp.where(inner > 0, hy, 1)
        rim_there = jnp.where(inner > 0, 0, hy + 1)
        rim_here = jnp.where(inner > 0, hy + 1, 0)
        every = pl.ds(1, ngx * hx)
        dst = strip.at[every, pl.ds(rim_there if sending else rim_here, 1)]
        src = strip.at[every, pl.ds(mine, 1)] if sending else dst
        return remote(src, dst, share_send, share_recv, g, mate)

    share(True).start()

    @pl.when(has_beyond)
    def _():
        for p in range(ngx):
            outer_in(p).wait_recv()

    fine_rows(late, 3)
    coarse_rows(jnp.where(inner > 0, 0, cy), 2)

    @pl.when(jnp.logical_not(has_beyond))
    def _():
        at_rim = pl.ds(jnp.where(inner > 0, 0, hy + 1), 1)
        strip[1 : ngx * hx + 1, at_rim] = jnp.zeros((ngx * hx, 1, depth, cd), BF16)

    share(False).wait_recv()
    for load in loads[5:]:
        load.wait()

    def swap(to, source):
        return remote(sent.at[to], back.at[source], swap_send.at[to], swap_recv.at[source], to, q)

    rows = hx * hy * depth

    @pl.loop(0, ngx - 1)
    def _(turn):
        n = ngx - 2 - turn
        step = jnp.where(n % 2 == 1, (n + 1) // 2, -((n + 1) // 2))
        at = g // 2 + step
        last = ngx // 2 - 1

        @pl.when(jnp.logical_and(at >= 0, at <= last))
        def _():
            def taps(j, k):
                return [
                    jnp.dot(
                        strip[pl.ds(2 * hx * at + i, 2 * hx), j : j + hy].reshape(2 * rows, cd),
                        bk[9 * i + 3 * j + k],
                        preferred_element_type=F32,
                    )
                    for i in range(3)
                ]

            for k in range(3):
                acc[k] = sum(taps(0, k) + taps(1, k) + taps(2, k))
            bottle = acc[1] + shifted(acc[0], 1, depth) + shifted(acc[2], -1, depth)
            bottle = silu(bottle + bb_ref[...]).astype(BF16)
            for i in range(2):
                p = 2 * at + i
                sent[p] = bottle[i * rows : (i + 1) * rows]
                pl.when(p != g)(swap(p, g).start)

    lifted = jnp.dot(sent[g], uk[g], preferred_element_type=F32)
    for d in range(1, ngx):
        source = lax.rem(g + d, ngx)
        swap(source, source).wait_recv()
        lifted += jnp.dot(back[source], uk[source], preferred_element_type=F32)
    ub = ub_ref[...]
    ub = jnp.concatenate([ub, ub], axis=1)
    for x in range(hx):
        for dx in (0, 1):
            columns = []
            for y in range(hy):
                at = (x * hy + y) * depth
                for dy in (0, 1):
                    c = (2 * dx + dy) * pair
                    columns.append(
                        fine_ref[cx * g + 2 * x + dx, 2 + 2 * y + dy].astype(F32)
                        + (lifted[at : at + depth, c : c + pair] + ub)
                    )
            whole = jnp.stack(columns).reshape(cy, depth * pair)
            out_ref[2 * x + dx] = whole.astype(BF16)

    def left(p):
        block(g, p).wait_send()
        swap(p, g).wait_send()

    others(left, near)
    for p in range(ngx):
        pl.when(has_beyond)(outer_out(p).wait_send)
        inner_out(p).wait_send()
    share(True).wait_send()


def local(
    sizes,
    volume,
    fine_kernel,
    fine_bias,
    down_kernel,
    down_bias,
    bottle_kernel,
    bottle_bias,
    up_kernel,
    up_bias,
):
    ngx = sizes[0]
    cx, cy, merged = volume.shape
    chans = fine_kernel.shape[1]
    pair = 2 * chans
    depth = merged // pair
    hx, hy = cx // 2, cy // 2
    cd = down_kernel.shape[1]
    cb = bottle_kernel.shape[2]
    cells = hx * hy * depth
    hbm = pl.BlockSpec(memory_space=pltpu.HBM)
    vmem = pl.BlockSpec(memory_space=pltpu.VMEM)
    dma = pltpu.SemaphoreType.DMA
    call = pl.pallas_call(
        functools.partial(body, sizes),
        out_shape=jax.ShapeDtypeStruct((cx, cy, merged), BF16),
        in_specs=[hbm] * 9,
        out_specs=vmem,
        scratch_shapes=[
            pltpu.VMEM(volume.shape, BF16),
            pltpu.VMEM((ngx * cx + 2, cy + 6, depth, pair), BF16),
            pltpu.VMEM(fine_kernel.shape, BF16),
            pltpu.VMEM((9 * pair, 2 * pair), BF16),
            pltpu.VMEM(down_kernel.shape, BF16),
            pltpu.VMEM(bottle_kernel.shape, BF16),
            pltpu.VMEM((ngx, cb, up_kernel.shape[1]), BF16),
            pltpu.VMEM((1, chans), F32),
            pltpu.VMEM((1, cd), F32),
            pltpu.VMEM((1, cb), F32),
            pltpu.VMEM((1, chans), F32),
            pltpu.VMEM((ngx * cx, cy + 4, depth, pair), BF16),
            pltpu.VMEM((ngx * hx + 2, hy + 2, depth, cd), BF16),
            pltpu.VMEM((3, 2 * cells, cb), F32),
            pltpu.VMEM((ngx, cells, cb), BF16),
            pltpu.VMEM((ngx, cells, cb), BF16),
            dma((17,)),
            dma((ngx,)),
            dma((ngx,)),
            dma((ngx,)),
            dma((ngx,)),
            dma((ngx,)),
            dma((ngx,)),
            dma((ngx,)),
            dma((ngx,)),
            dma,
            dma,
        ],
        compiler_params=pltpu.CompilerParams(
            collective_id=0, has_side_effects=True, vmem_limit_bytes=52 << 20
        ),
    )
    arrays = (
        volume,
        fine_kernel,
        fine_bias.reshape(1, -1),
        down_kernel,
        down_bias.reshape(1, -1),
        bottle_kernel,
        bottle_bias.reshape(1, -1),
        up_kernel.reshape(ngx, cb, -1),
        up_bias.reshape(1, -1),
    )
    return call(*(pltpu.with_memory_space_constraint(a, pltpu.HBM) for a in arrays))


def solution(mesh):
    placed = (
        P(("groups", "gx"), ("gy", "col"), None),
        P(),
        P(),
        P(),
        P(),
        P(None, None, "gx"),
        P("gx"),
        P(),
        P(),
    )
    sizes = tuple(mesh.shape[name] for name in ("gx", "gy", "col"))
    return jax.shard_map(
        functools.partial(local, sizes),
        mesh=mesh,
        in_specs=placed,
        out_specs=P(("groups", "gx"), ("gy", "col"), None),
        check_vma=False,
    )
```

```python
import functools

import jax
import jax.numpy as jnp
from jax import lax
from jax.experimental import pallas as pl
from jax.experimental.pallas import tpu as pltpu
from jax.sharding import PartitionSpec as P

MESH = pl.DeviceIdType.MESH
F32 = jnp.float32
BF16 = jnp.bfloat16
PARTS = 2


def silu(a):
    return (0.5 * a) * (1.0 + jnp.tanh(0.5 * a))


def shifted(a, amount, depth):
    rows = a.shape[0]
    z = lax.broadcasted_iota(jnp.int32, a.shape, 0) % depth
    moved = pltpu.roll(a, amount % rows, 0)
    keep = z >= amount if amount > 0 else z < depth + amount
    return jnp.where(keep, moved, 0.0)


def body(
    sizes,
    vol_hbm,
    fk_hbm,
    fb_hbm,
    dk_hbm,
    db_hbm,
    bk_hbm,
    bb_hbm,
    uk_hbm,
    ub_hbm,
    out_ref,
    raw,
    brick,
    fk,
    band,
    dk,
    bk,
    uk,
    fb_ref,
    db_ref,
    bb_ref,
    ub_ref,
    fine_ref,
    strip,
    acc,
    sent,
    back,
    word,
    load_sem,
    block_send,
    block_recv,
    outer_send,
    outer_recv,
    inner_send,
    inner_recv,
    swap_send,
    swap_recv,
    share_send,
    share_recv,
):
    ngx, ngy, ncol = sizes
    nq = ngy * ncol
    cx, cy = raw.shape[:2]
    depth, pair = fine_ref.shape[2:]
    chans = pair // 2
    hx, hy = cx // 2, cy // 2
    cd = dk.shape[1]
    cb = bk.shape[2]
    g = lax.axis_index("gx")
    col = lax.axis_index("col")
    q = lax.axis_index("gy") * ncol + col

    def device(gg, qq):
        return {"gx": gg, "gy": qq // ncol, "col": qq % ncol}

    loads = [
        pltpu.make_async_copy(src, dst, load_sem.at[n])
        for n, (src, dst) in enumerate(
            (
                (vol_hbm, raw),
                (fk_hbm, fk),
                (fb_hbm, fb_ref),
                (dk_hbm, dk),
                (db_hbm, db_ref),
                (bb_hbm, bb_ref),
                (uk_hbm, uk),
                (ub_hbm, ub_ref),
            )
            + tuple((bk_hbm.at[pl.ds(3 * n, 3)], bk.at[pl.ds(3 * n, 3)]) for n in range(9))
        )
    ]
    for load in loads:
        load.start()

    rim = 3
    half = cy // 2 + 2
    brick[0] = jnp.zeros_like(brick[0])
    brick[ngx * cx + 1] = jnp.zeros_like(brick[0])
    strip[0] = jnp.zeros_like(strip[0])
    strip[ngx * hx + 1] = jnp.zeros_like(strip[0])

    @pl.when(q == 0)
    def _():
        brick[1 : ngx * cx + 1, :rim] = jnp.zeros((ngx * cx, rim, depth, pair), BF16)

    @pl.when(q == nq - 1)
    def _():
        brick[1 : ngx * cx + 1, rim + cy :] = jnp.zeros((ngx * cx, rim, depth, pair), BF16)

    def valid(gg, qq):
        ok = jnp.logical_and(gg >= 0, gg < ngx)
        return jnp.logical_and(ok, jnp.logical_and(qq >= 0, qq < nq))

    barrier = pltpu.get_barrier_semaphore()

    def greet(gg, qq):
        pl.semaphore_signal(barrier, inc=1, device_id=device(gg, qq), device_id_type=MESH)

    inner = 1 - 2 * col
    mate = q + inner
    beyond = q - inner
    has_beyond = valid(g, beyond)
    partners = 1 + has_beyond.astype(jnp.int32)
    for p in (g - 1, g + 1):
        there = valid(p, q)
        pl.when(there)(functools.partial(greet, p, q))
        partners += there.astype(jnp.int32)
    greet(g, mate)
    pl.when(has_beyond)(functools.partial(greet, g, beyond))

    loads[0].wait()
    for x in range(cx):
        brick[1 + cx * g + x, rim : rim + cy] = (
            raw[x].astype(F32).reshape(cy, depth, pair).astype(BF16)
        )
    pl.semaphore_wait(barrier, partners)

    def remote(src, dst, send, recv, gg, qq):
        return pltpu.make_async_remote_copy(
            src_ref=src,
            dst_ref=dst,
            send_sem=send,
            recv_sem=recv,
            device_id=device(gg, qq),
            device_id_type=MESH,
        )

    def layers(at):
        return pl.ds(1 + cx * at, cx)

    part = cx // PARTS

    def slab(at, n):
        return pl.ds(1 + cx * at + part * n, part)

    def block(source, to, n):
        ref = brick.at[slab(source, n), pl.ds(rim, cy)]
        return remote(ref, ref, block_send.at[to, n], block_recv.at[source, n], to, q)

    def rows_out(xs, b, count, send, recv, beside):
        src = jnp.where(b > 0, rim + cy - count, rim)
        dst = jnp.where(b > 0, rim - count, rim + cy)
        return remote(
            brick.at[xs, pl.ds(src, count)], brick.at[xs, pl.ds(dst, count)], send, recv, g, beside
        )

    def rows_in(xs, b, count, send, recv, beside):
        ref = brick.at[xs, pl.ds(jnp.where(b > 0, rim + cy, rim - count), count)]
        return remote(ref, ref, send, recv, g, beside)

    def inner_out(at):
        return rows_out(layers(at), inner, 1, inner_send.at[at], inner_recv.at[at], mate)

    def inner_in(at):
        return rows_in(layers(at), inner, 1, inner_send.at[at], inner_recv.at[at], mate)

    def outer_out(at, n):
        return rows_out(slab(at, n), -inner, rim, outer_send.at[at, n], outer_recv.at[at, n], beyond)

    def outer_in(at, n):
        return rows_in(slab(at, n), -inner, rim, outer_send.at[at, n], outer_recv.at[at, n], beyond)

    def others(visit, order):
        for d in order:
            for p in (g + d, g - d):
                pl.when(valid(p, q))(functools.partial(visit, p))

    near = tuple(range(1, ngx))

    def send(p):
        for n in range(PARTS):
            block(g, p, n).start()

    def tell(side):
        pl.semaphore_signal(
            word.at[side], inc=1, device_id=device(g + 2 * side - 1, q), device_id_type=MESH
        )

    between = jnp.logical_and(g > 0, g < ngx - 1)
    for side in (0, 1):
        pl.when(between)(functools.partial(tell, side))
    others(send, (1,))
    for n in range(PARTS):
        pl.when(has_beyond)(outer_out(g, n).start)
    inner_out(g).start()
    for d in range(2, ngx):
        for side in (0, 1):
            p = g + d if side == 0 else g - d

            @pl.when(valid(p, q))
            def _():
                pl.semaphore_wait(word.at[side], 1)
                send(p)
                pl.when(g > 0 if side == 0 else g < ngx - 1)(functools.partial(tell, side))


    loads[1].wait()
    empty = jnp.zeros((chans, chans), BF16)
    for ij in range(9):
        f0, f1, f2 = fk[3 * ij], fk[3 * ij + 1], fk[3 * ij + 2]
        band[ij * pair : ij * pair + chans] = jnp.concatenate([f1, f0, empty, f2], axis=1)
        band[ij * pair + chans : (ij + 1) * pair] = jnp.concatenate([f2, f1, f0, empty], axis=1)

    def arrive(p):
        for n in range(PARTS):
            block(p, p, n).wait_recv()
            pl.when(has_beyond)(outer_out(p, n).start)
        inner_out(p).start()

    others(arrive, near)
    for load in loads[2:5]:
        load.wait()
    for p in range(ngx):
        inner_in(p).wait_recv()

    group = 2
    bunch = min(ngx, 4)

    def fine_rows(top, count, n):
        layer = group * cx * n
        pieces = [
            brick[pl.ds(layer + i, group * cx), pl.ds(top + j, count)].reshape(group * cx * count * depth, pair)
            for i in range(3)
            for j in range(3)
        ]
        prod = jnp.dot(jnp.concatenate(pieces, axis=1), band[...], preferred_element_type=F32)
        wing = prod[:, pair:]
        lane = lax.broadcasted_iota(jnp.int32, wing.shape, 1)
        fb = fb_ref[...]
        total = (
            prod[:, :pair]
            + jnp.where(lane < chans, shifted(wing, 1, depth), shifted(wing, -1, depth))
            + jnp.concatenate([fb, fb], axis=1)
        )
        fine = silu(total).astype(BF16).reshape(group * cx, count, depth, pair)
        fine_ref[pl.ds(layer, group * cx), pl.ds(top, count)] = fine

    def coarse_rows(top, count):
        @pl.loop(0, ngx // bunch)
        def _(n):
            fine = fine_ref[pl.ds(bunch * cx * n, bunch * cx), pl.ds(top, 2 * count)]
            cells = [
                jnp.concatenate(
                    [fine[2 * x + dx, 2 * y + dy] for dx in (0, 1) for dy in (0, 1)], axis=1
                )
                for x in range(bunch * hx)
                for y in range(count)
            ]
            coarse = jnp.dot(jnp.concatenate(cells, axis=0), dk[...], preferred_element_type=F32)
            coarse = silu(coarse + db_ref[...]).astype(BF16)
            strip[pl.ds(1 + bunch * hx * n, bunch * hx), pl.ds(top // 2, count)] = coarse.reshape(
                bunch * hx, count, depth, cd
            )

    early = jnp.where(inner > 0, 3, 2)
    late = jnp.where(inner > 0, 0, cy + 1)
    pl.loop(0, ngx // group)(functools.partial(fine_rows, early, cy - 1))
    coarse_rows(jnp.where(inner > 0, 4, 2), hy - 1)

    def share(sending):
        mine = jnp.where(inner > 0, hy, 1)
        rim_there = jnp.where(inner > 0, 0, hy + 1)
        rim_here = jnp.where(inner > 0, hy + 1, 0)
        every = pl.ds(1, ngx * hx)
        dst = strip.at[every, pl.ds(rim_there if sending else rim_here, 1)]
        src = strip.at[every, pl.ds(mine, 1)] if sending else dst
        return remote(src, dst, share_send, share_recv, g, mate)

    share(True).start()

    def steps(visit):
        @pl.loop(0, ngx - 1)
        def _(n):
            step = jnp.where(n % 2 == 1, (n + 1) // 2, -((n + 1) // 2))
            at = g // 2 + step
            pl.when(jnp.logical_and(at >= 0, at < ngx // 2))(functools.partial(visit, step, at))

    def late_rows(step, at):
        low = jnp.where(step > 0, 2 * at + 1, 2 * at - 1)
        high = jnp.where(step < 0, 2 * at, 2 * at + 2)
        for i in range(-1, 3):
            p = 2 * at + i
            new = jnp.logical_and(p >= low, p <= high)

            @pl.when(jnp.logical_and(has_beyond, jnp.logical_and(new, valid(p, q))))
            def _():
                for n in range(PARTS):
                    outer_in(p, n).wait_recv()

        fine_rows(late, 3, at)

    steps(late_rows)
    coarse_rows(jnp.where(inner > 0, 0, cy), 2)

    @pl.when(jnp.logical_not(has_beyond))
    def _():
        at_rim = pl.ds(jnp.where(inner > 0, 0, hy + 1), 1)
        strip[1 : ngx * hx + 1, at_rim] = jnp.zeros((ngx * hx, 1, depth, cd), BF16)

    share(False).wait_recv()
    for load in loads[5:]:
        load.wait()

    def swap(to, source):
        return remote(sent.at[to], back.at[source], swap_send.at[to], swap_recv.at[source], to, q)

    rows = hx * hy * depth

    @pl.loop(0, ngx - 1)
    def _(turn):
        n = ngx - 2 - turn
        step = jnp.where(n % 2 == 1, (n + 1) // 2, -((n + 1) // 2))
        at = g // 2 + step
        last = ngx // 2 - 1

        @pl.when(jnp.logical_and(at >= 0, at <= last))
        def _():
            def taps(j, k):
                return [
                    jnp.dot(
                        strip[pl.ds(2 * hx * at + i, 2 * hx), j : j + hy].reshape(2 * rows, cd),
                        bk[9 * i + 3 * j + k],
                        preferred_element_type=F32,
                    )
                    for i in range(3)
                ]

            for k in range(3):
                acc[k] = sum(taps(0, k) + taps(1, k) + taps(2, k))
            bottle = acc[1] + shifted(acc[0], 1, depth) + shifted(acc[2], -1, depth)
            bottle = silu(bottle + bb_ref[...]).astype(BF16)
            for i in range(2):
                p = 2 * at + i
                sent[p] = bottle[i * rows : (i + 1) * rows]
                pl.when(p != g)(swap(p, g).start)

    lifted = jnp.dot(sent[g], uk[g], preferred_element_type=F32)
    for d in range(1, ngx):
        source = lax.rem(g + d, ngx)
        swap(source, source).wait_recv()
        lifted += jnp.dot(back[source], uk[source], preferred_element_type=F32)
    ub = ub_ref[...]
    ub = jnp.concatenate([ub, ub], axis=1)
    for x in range(hx):
        for dx in (0, 1):
            columns = []
            for y in range(hy):
                at = (x * hy + y) * depth
                for dy in (0, 1):
                    c = (2 * dx + dy) * pair
                    columns.append(
                        fine_ref[cx * g + 2 * x + dx, 2 + 2 * y + dy].astype(F32)
                        + (lifted[at : at + depth, c : c + pair] + ub)
                    )
            whole = jnp.stack(columns).reshape(cy, depth * pair)
            out_ref[2 * x + dx] = whole.astype(BF16)

    def left(p):
        for n in range(PARTS):
            block(g, p, n).wait_send()
        swap(p, g).wait_send()

    others(left, near)
    for p in range(ngx):
        for n in range(PARTS):
            pl.when(has_beyond)(outer_out(p, n).wait_send)
        inner_out(p).wait_send()
    share(True).wait_send()


def local(
    sizes,
    volume,
    fine_kernel,
    fine_bias,
    down_kernel,
    down_bias,
    bottle_kernel,
    bottle_bias,
    up_kernel,
    up_bias,
):
    ngx = sizes[0]
    cx, cy, merged = volume.shape
    chans = fine_kernel.shape[1]
    pair = 2 * chans
    depth = merged // pair
    hx, hy = cx // 2, cy // 2
    cd = down_kernel.shape[1]
    cb = bottle_kernel.shape[2]
    cells = hx * hy * depth
    hbm = pl.BlockSpec(memory_space=pltpu.HBM)
    vmem = pl.BlockSpec(memory_space=pltpu.VMEM)
    dma = pltpu.SemaphoreType.DMA
    call = pl.pallas_call(
        functools.partial(body, sizes),
        out_shape=jax.ShapeDtypeStruct((cx, cy, merged), BF16),
        in_specs=[hbm] * 9,
        out_specs=vmem,
        scratch_shapes=[
            pltpu.VMEM(volume.shape, BF16),
            pltpu.VMEM((ngx * cx + 2, cy + 6, depth, pair), BF16),
            pltpu.VMEM(fine_kernel.shape, BF16),
            pltpu.VMEM((9 * pair, 2 * pair), BF16),
            pltpu.VMEM(down_kernel.shape, BF16),
            pltpu.VMEM(bottle_kernel.shape, BF16),
            pltpu.VMEM((ngx, cb, up_kernel.shape[1]), BF16),
            pltpu.VMEM((1, chans), F32),
            pltpu.VMEM((1, cd), F32),
            pltpu.VMEM((1, cb), F32),
            pltpu.VMEM((1, chans), F32),
            pltpu.VMEM((ngx * cx, cy + 4, depth, pair), BF16),
            pltpu.VMEM((ngx * hx + 2, hy + 2, depth, cd), BF16),
            pltpu.VMEM((3, 2 * cells, cb), F32),
            pltpu.VMEM((ngx, cells, cb), BF16),
            pltpu.VMEM((ngx, cells, cb), BF16),
            pltpu.SemaphoreType.REGULAR((2,)),
            dma((17,)),
            dma((ngx, PARTS)),
            dma((ngx, PARTS)),
            dma((ngx, PARTS)),
            dma((ngx, PARTS)),
            dma((ngx,)),
            dma((ngx,)),
            dma((ngx,)),
            dma((ngx,)),
            dma,
            dma,
        ],
        compiler_params=pltpu.CompilerParams(
            collective_id=0, has_side_effects=True, vmem_limit_bytes=52 << 20
        ),
    )
    arrays = (
        volume,
        fine_kernel,
        fine_bias.reshape(1, -1),
        down_kernel,
        down_bias.reshape(1, -1),
        bottle_kernel,
        bottle_bias.reshape(1, -1),
        up_kernel.reshape(ngx, cb, -1),
        up_bias.reshape(1, -1),
    )
    return call(*(pltpu.with_memory_space_constraint(a, pltpu.HBM) for a in arrays))


def solution(mesh):
    placed = (
        P(("groups", "gx"), ("gy", "col"), None),
        P(),
        P(),
        P(),
        P(),
        P(None, None, "gx"),
        P("gx"),
        P(),
        P(),
    )
    sizes = tuple(mesh.shape[name] for name in ("gx", "gy", "col"))
    return jax.shard_map(
        functools.partial(local, sizes),
        mesh=mesh,
        in_specs=placed,
        out_specs=P(("groups", "gx"), ("gy", "col"), None),
        check_vma=False,
    )
```

```python
import functools

import jax
import jax.numpy as jnp
from jax import lax
from jax.experimental import pallas as pl
from jax.experimental.pallas import tpu as pltpu
from jax.sharding import PartitionSpec as P

MESH = pl.DeviceIdType.MESH
F32 = jnp.float32
BF16 = jnp.bfloat16
PARTS = 2


def silu(a):
    return (0.5 * a) * (1.0 + jnp.tanh(0.5 * a))


def shifted(a, amount, depth):
    rows = a.shape[0]
    z = lax.broadcasted_iota(jnp.int32, a.shape, 0) % depth
    moved = pltpu.roll(a, amount % rows, 0)
    keep = z >= amount if amount > 0 else z < depth + amount
    return jnp.where(keep, moved, 0.0)


def body(
    sizes,
    vol_hbm,
    fk_hbm,
    fb_hbm,
    dk_hbm,
    db_hbm,
    bk_hbm,
    bb_hbm,
    uk_hbm,
    ub_hbm,
    out_ref,
    raw,
    brick,
    fk,
    band,
    dk,
    bk,
    uk,
    fb_ref,
    db_ref,
    bb_ref,
    ub_ref,
    fine_ref,
    strip,
    acc,
    sent,
    back,
    word,
    load_sem,
    block_send,
    block_recv,
    outer_send,
    outer_recv,
    inner_send,
    inner_recv,
    swap_send,
    swap_recv,
    share_send,
    share_recv,
    base,
):
    ngx, ngy, ncol = sizes
    nq = ngy * ncol
    cx, cy = raw.shape[:2]
    depth, pair = fine_ref.shape[2:]
    chans = pair // 2
    hx, hy = cx // 2, cy // 2
    cd = dk.shape[1]
    cb = bk.shape[2]
    g = lax.axis_index("gx")
    col = lax.axis_index("col")
    q = lax.axis_index("gy") * ncol + col

    def device(gg, qq):
        return {"gx": gg, "gy": qq // ncol, "col": qq % ncol}

    loads = [
        pltpu.make_async_copy(src, dst, load_sem.at[n])
        for n, (src, dst) in enumerate(
            (
                (vol_hbm, raw),
                (fk_hbm, fk),
                (fb_hbm, fb_ref),
                (dk_hbm, dk),
                (db_hbm, db_ref),
                (bb_hbm, bb_ref),
                (uk_hbm, uk),
                (ub_hbm, ub_ref),
            )
            + tuple((bk_hbm.at[pl.ds(3 * n, 3)], bk.at[pl.ds(3 * n, 3)]) for n in range(9))
        )
    ]
    loads[0].start()

    rim = 3

    def valid(gg, qq):
        ok = jnp.logical_and(gg >= 0, gg < ngx)
        return jnp.logical_and(ok, jnp.logical_and(qq >= 0, qq < nq))

    barrier = pltpu.get_barrier_semaphore()

    def greet(gg, qq):
        pl.semaphore_signal(barrier, inc=1, device_id=device(gg, qq), device_id_type=MESH)

    inner = 1 - 2 * col
    mate = q + inner
    beyond = q - inner
    has_beyond = valid(g, beyond)
    partners = 1 + has_beyond.astype(jnp.int32)
    for p in (g - 1, g + 1):
        there = valid(p, q)
        pl.when(there)(functools.partial(greet, p, q))
        partners += there.astype(jnp.int32)
    greet(g, mate)
    pl.when(has_beyond)(functools.partial(greet, g, beyond))

    loads[0].wait()
    for x in range(cx):
        brick[1 + cx * g + x, rim : rim + cy] = (
            raw[x].astype(F32).reshape(cy, depth, pair).astype(BF16)
        )
    pl.semaphore_wait(barrier, partners)

    def remote(src, dst, send, recv, gg, qq):
        return pltpu.make_async_remote_copy(
            src_ref=src,
            dst_ref=dst,
            send_sem=send,
            recv_sem=recv,
            device_id=device(gg, qq),
            device_id_type=MESH,
        )

    def layers(at):
        return pl.ds(1 + cx * at, cx)

    part = cx // PARTS

    def slab(at, n):
        return pl.ds(1 + cx * at + part * n, part)

    def block(source, to, n):
        ref = brick.at[slab(source, n), pl.ds(rim, cy)]
        return remote(ref, ref, block_send.at[to, n], block_recv.at[source, n], to, q)

    def rows_out(xs, b, count, send, recv, beside):
        src = jnp.where(b > 0, rim + cy - count, rim)
        dst = jnp.where(b > 0, rim - count, rim + cy)
        return remote(
            brick.at[xs, pl.ds(src, count)], brick.at[xs, pl.ds(dst, count)], send, recv, g, beside
        )

    def rows_in(xs, b, count, send, recv, beside):
        ref = brick.at[xs, pl.ds(jnp.where(b > 0, rim + cy, rim - count), count)]
        return remote(ref, ref, send, recv, g, beside)

    def inner_out(at):
        return rows_out(layers(at), inner, 1, inner_send.at[at], inner_recv.at[at], mate)

    def inner_in(at):
        return rows_in(layers(at), inner, 1, inner_send.at[at], inner_recv.at[at], mate)

    def outer_out(at, n):
        return rows_out(slab(at, n), -inner, rim, outer_send.at[at, n], outer_recv.at[at, n], beyond)

    def outer_in(at, n):
        return rows_in(slab(at, n), -inner, rim, outer_send.at[at, n], outer_recv.at[at, n], beyond)

    def others(visit, order):
        for d in order:
            for p in (g + d, g - d):
                pl.when(valid(p, q))(functools.partial(visit, p))

    near = tuple(range(1, ngx))

    def send(p):
        for n in range(PARTS):
            block(g, p, n).start()

    def tell(side):
        pl.semaphore_signal(
            word.at[side], inc=1, device_id=device(g + 2 * side - 1, q), device_id_type=MESH
        )

    between = jnp.logical_and(g > 0, g < ngx - 1)
    for side in (0, 1):
        pl.when(between)(functools.partial(tell, side))
    others(send, (1,))
    for n in range(PARTS):
        pl.when(has_beyond)(outer_out(g, n).start)
    inner_out(g).start()
    for d in range(2, ngx):
        for side in (0, 1):
            p = g + d if side == 0 else g - d

            @pl.when(valid(p, q))
            def _():
                pl.semaphore_wait(word.at[side], 1)
                send(p)
                pl.when(g > 0 if side == 0 else g < ngx - 1)(functools.partial(tell, side))


    for load in loads[1:]:
        load.start()
    half = cy // 2 + 2
    brick[0] = jnp.zeros_like(brick[0])
    brick[ngx * cx + 1] = jnp.zeros_like(brick[0])
    strip[0] = jnp.zeros_like(strip[0])
    strip[ngx * hx + 1] = jnp.zeros_like(strip[0])

    @pl.when(q == 0)
    def _():
        brick[1 : ngx * cx + 1, :rim] = jnp.zeros((ngx * cx, rim, depth, pair), BF16)

    @pl.when(q == nq - 1)
    def _():
        brick[1 : ngx * cx + 1, rim + cy :] = jnp.zeros((ngx * cx, rim, depth, pair), BF16)

    loads[1].wait()
    empty = jnp.zeros((chans, chans), BF16)
    for ij in range(9):
        f0, f1, f2 = fk[3 * ij], fk[3 * ij + 1], fk[3 * ij + 2]
        band[ij * pair : ij * pair + chans] = jnp.concatenate([f1, f0, empty, f2], axis=1)
        band[ij * pair + chans : (ij + 1) * pair] = jnp.concatenate([f2, f1, f0, empty], axis=1)

    def arrive(p):
        for n in range(PARTS):
            block(p, p, n).wait_recv()
            pl.when(has_beyond)(outer_out(p, n).start)
        inner_out(p).start()

    others(arrive, near)
    for load in loads[2:5]:
        load.wait()
    for p in range(ngx):
        inner_in(p).wait_recv()

    group = 2
    bunch = min(ngx, 4)

    def fine_rows(top, count, n):
        layer = group * cx * n
        pieces = [
            brick[pl.ds(layer + i, group * cx), pl.ds(top + j, count)].reshape(group * cx * count * depth, pair)
            for i in range(3)
            for j in range(3)
        ]
        prod = jnp.dot(jnp.concatenate(pieces, axis=1), band[...], preferred_element_type=F32)
        wing = prod[:, pair:]
        lane = lax.broadcasted_iota(jnp.int32, wing.shape, 1)
        fb = fb_ref[...]
        total = (
            prod[:, :pair]
            + jnp.where(lane < chans, shifted(wing, 1, depth), shifted(wing, -1, depth))
            + jnp.concatenate([fb, fb], axis=1)
        )
        fine = silu(total).astype(BF16).reshape(group * cx, count, depth, pair)
        fine_ref[pl.ds(layer, group * cx), pl.ds(top, count)] = fine

    def coarse_rows(top, count):
        @pl.loop(0, ngx // bunch)
        def _(n):
            fine = fine_ref[pl.ds(bunch * cx * n, bunch * cx), pl.ds(top, 2 * count)]
            cells = [
                jnp.concatenate(
                    [fine[2 * x + dx, 2 * y + dy] for dx in (0, 1) for dy in (0, 1)], axis=1
                )
                for x in range(bunch * hx)
                for y in range(count)
            ]
            coarse = jnp.dot(jnp.concatenate(cells, axis=0), dk[...], preferred_element_type=F32)
            coarse = silu(coarse + db_ref[...]).astype(BF16)
            strip[pl.ds(1 + bunch * hx * n, bunch * hx), pl.ds(top // 2, count)] = coarse.reshape(
                bunch * hx, count, depth, cd
            )

    early = jnp.where(inner > 0, 3, 2)
    late = jnp.where(inner > 0, 0, cy + 1)
    pl.loop(0, ngx // group)(functools.partial(fine_rows, early, cy - 1))
    coarse_rows(jnp.where(inner > 0, 4, 2), hy - 1)

    def share(sending):
        mine = jnp.where(inner > 0, hy, 1)
        rim_there = jnp.where(inner > 0, 0, hy + 1)
        rim_here = jnp.where(inner > 0, hy + 1, 0)
        every = pl.ds(1, ngx * hx)
        dst = strip.at[every, pl.ds(rim_there if sending else rim_here, 1)]
        src = strip.at[every, pl.ds(mine, 1)] if sending else dst
        return remote(src, dst, share_send, share_recv, g, mate)

    share(True).start()

    def steps(visit):
        @pl.loop(0, ngx - 1)
        def _(n):
            step = jnp.where(n % 2 == 1, (n + 1) // 2, -((n + 1) // 2))
            at = g // 2 + step
            pl.when(jnp.logical_and(at >= 0, at < ngx // 2))(functools.partial(visit, step, at))

    def late_rows(step, at):
        low = jnp.where(step > 0, 2 * at + 1, 2 * at - 1)
        high = jnp.where(step < 0, 2 * at, 2 * at + 2)
        for i in range(-1, 3):
            p = 2 * at + i
            new = jnp.logical_and(p >= low, p <= high)

            @pl.when(jnp.logical_and(has_beyond, jnp.logical_and(new, valid(p, q))))
            def _():
                for n in range(PARTS):
                    outer_in(p, n).wait_recv()

        fine_rows(late, 3, at)

    steps(late_rows)
    coarse_rows(jnp.where(inner > 0, 0, cy), 2)

    @pl.when(jnp.logical_not(has_beyond))
    def _():
        at_rim = pl.ds(jnp.where(inner > 0, 0, hy + 1), 1)
        strip[1 : ngx * hx + 1, at_rim] = jnp.zeros((ngx * hx, 1, depth, cd), BF16)

    share(False).wait_recv()
    for load in loads[5:]:
        load.wait()

    def swap(to, source):
        return remote(sent.at[to], back.at[source], swap_send.at[to], swap_recv.at[source], to, q)

    rows = hx * hy * depth

    @pl.loop(0, ngx - 1)
    def _(turn):
        n = ngx - 2 - turn
        step = jnp.where(n % 2 == 1, (n + 1) // 2, -((n + 1) // 2))
        at = g // 2 + step
        last = ngx // 2 - 1

        @pl.when(jnp.logical_and(at >= 0, at <= last))
        def _():
            def taps(j, k):
                return [
                    jnp.dot(
                        strip[pl.ds(2 * hx * at + i, 2 * hx), j : j + hy].reshape(2 * rows, cd),
                        bk[9 * i + 3 * j + k],
                        preferred_element_type=F32,
                    )
                    for i in range(3)
                ]

            for k in range(3):
                acc[k] = sum(taps(0, k) + taps(1, k) + taps(2, k))
            bottle = acc[1] + shifted(acc[0], 1, depth) + shifted(acc[2], -1, depth)
            bottle = silu(bottle + bb_ref[...]).astype(BF16)
            for i in range(2):
                p = 2 * at + i
                sent[p] = bottle[i * rows : (i + 1) * rows]
                pl.when(p != g)(swap(p, g).start)

    ub = ub_ref[...]
    ub = jnp.concatenate([ub, ub], axis=1)
    lifted = jnp.dot(sent[g], uk[g], preferred_element_type=F32) + jnp.concatenate([ub] * 4, axis=1)
    for x in range(hx):
        for dx in (0, 1):
            for y in range(hy):
                at = (x * hy + y) * depth
                for dy in (0, 1):
                    c = (2 * dx + dy) * pair
                    base[at : at + depth, c : c + pair] = (
                        fine_ref[cx * g + 2 * x + dx, 2 + 2 * y + dy].astype(F32)
                        + lifted[at : at + depth, c : c + pair]
                    )
    for d in range(1, ngx - 1):
        source = lax.rem(g + d, ngx)
        swap(source, source).wait_recv()
        base[...] += jnp.dot(back[source], uk[source], preferred_element_type=F32)
    source = lax.rem(g + ngx - 1, ngx)
    swap(source, source).wait_recv()
    lifted = base[...] + jnp.dot(back[source], uk[source], preferred_element_type=F32)
    for x in range(hx):
        for dx in (0, 1):
            columns = []
            for y in range(hy):
                at = (x * hy + y) * depth
                for dy in (0, 1):
                    c = (2 * dx + dy) * pair
                    columns.append(lifted[at : at + depth, c : c + pair])
            out_ref[2 * x + dx] = jnp.stack(columns).reshape(cy, depth * pair).astype(BF16)

    def left(p):
        for n in range(PARTS):
            block(g, p, n).wait_send()
        swap(p, g).wait_send()

    others(left, near)
    for p in range(ngx):
        for n in range(PARTS):
            pl.when(has_beyond)(outer_out(p, n).wait_send)
        inner_out(p).wait_send()
    share(True).wait_send()


def local(
    sizes,
    volume,
    fine_kernel,
    fine_bias,
    down_kernel,
    down_bias,
    bottle_kernel,
    bottle_bias,
    up_kernel,
    up_bias,
):
    ngx = sizes[0]
    cx, cy, merged = volume.shape
    chans = fine_kernel.shape[1]
    pair = 2 * chans
    depth = merged // pair
    hx, hy = cx // 2, cy // 2
    cd = down_kernel.shape[1]
    cb = bottle_kernel.shape[2]
    cells = hx * hy * depth
    hbm = pl.BlockSpec(memory_space=pltpu.HBM)
    vmem = pl.BlockSpec(memory_space=pltpu.VMEM)
    dma = pltpu.SemaphoreType.DMA
    call = pl.pallas_call(
        functools.partial(body, sizes),
        out_shape=jax.ShapeDtypeStruct((cx, cy, merged), BF16),
        in_specs=[hbm] * 9,
        out_specs=vmem,
        scratch_shapes=[
            pltpu.VMEM(volume.shape, BF16),
            pltpu.VMEM((ngx * cx + 2, cy + 6, depth, pair), BF16),
            pltpu.VMEM(fine_kernel.shape, BF16),
            pltpu.VMEM((9 * pair, 2 * pair), BF16),
            pltpu.VMEM(down_kernel.shape, BF16),
            pltpu.VMEM(bottle_kernel.shape, BF16),
            pltpu.VMEM((ngx, cb, up_kernel.shape[1]), BF16),
            pltpu.VMEM((1, chans), F32),
            pltpu.VMEM((1, cd), F32),
            pltpu.VMEM((1, cb), F32),
            pltpu.VMEM((1, chans), F32),
            pltpu.VMEM((ngx * cx, cy + 4, depth, pair), BF16),
            pltpu.VMEM((ngx * hx + 2, hy + 2, depth, cd), BF16),
            pltpu.VMEM((3, 2 * cells, cb), F32),
            pltpu.VMEM((ngx, cells, cb), BF16),
            pltpu.VMEM((ngx, cells, cb), BF16),
            pltpu.SemaphoreType.REGULAR((2,)),
            dma((17,)),
            dma((ngx, PARTS)),
            dma((ngx, PARTS)),
            dma((ngx, PARTS)),
            dma((ngx, PARTS)),
            dma((ngx,)),
            dma((ngx,)),
            dma((ngx,)),
            dma((ngx,)),
            dma,
            dma,
            pltpu.VMEM((cells, up_kernel.shape[1]), F32),
        ],
        compiler_params=pltpu.CompilerParams(
            collective_id=0, has_side_effects=True, vmem_limit_bytes=52 << 20
        ),
    )
    arrays = (
        volume,
        fine_kernel,
        fine_bias.reshape(1, -1),
        down_kernel,
        down_bias.reshape(1, -1),
        bottle_kernel,
        bottle_bias.reshape(1, -1),
        up_kernel.reshape(ngx, cb, -1),
        up_bias.reshape(1, -1),
    )
    return call(*(pltpu.with_memory_space_constraint(a, pltpu.HBM) for a in arrays))


def solution(mesh):
    placed = (
        P(("groups", "gx"), ("gy", "col"), None),
        P(),
        P(),
        P(),
        P(),
        P(None, None, "gx"),
        P("gx"),
        P(),
        P(),
    )
    sizes = tuple(mesh.shape[name] for name in ("gx", "gy", "col"))
    return jax.shard_map(
        functools.partial(local, sizes),
        mesh=mesh,
        in_specs=placed,
        out_specs=P(("groups", "gx"), ("gy", "col"), None),
        check_vma=False,
    )
```

```python
import functools

import jax
import jax.numpy as jnp
from jax import lax
from jax.experimental import pallas as pl
from jax.experimental.pallas import tpu as pltpu
from jax.sharding import PartitionSpec as P

MESH = pl.DeviceIdType.MESH
F32 = jnp.float32
BF16 = jnp.bfloat16
PARTS = 2


def silu(a):
    return (0.5 * a) * (1.0 + jnp.tanh(0.5 * a))


def shifted(a, amount, depth):
    rows = a.shape[0]
    z = lax.broadcasted_iota(jnp.int32, a.shape, 0) % depth
    moved = pltpu.roll(a, amount % rows, 0)
    keep = z >= amount if amount > 0 else z < depth + amount
    return jnp.where(keep, moved, 0.0)


def body(
    sizes,
    vol_hbm,
    fk_hbm,
    fb_hbm,
    dk_hbm,
    db_hbm,
    bk_hbm,
    bb_hbm,
    uk_hbm,
    ub_hbm,
    out_ref,
    raw,
    brick,
    fk,
    band,
    dk,
    bk,
    uk,
    fb_ref,
    db_ref,
    bb_ref,
    ub_ref,
    fine_ref,
    strip,
    acc,
    sent,
    back,
    word,
    load_sem,
    block_send,
    block_recv,
    outer_send,
    outer_recv,
    inner_send,
    inner_recv,
    swap_send,
    swap_recv,
    share_send,
    share_recv,
    base,
):
    ngx, ngy, ncol = sizes
    nq = ngy * ncol
    cx, cy = raw.shape[:2]
    depth, pair = fine_ref.shape[2:]
    chans = pair // 2
    hx, hy = cx // 2, cy // 2
    cd = dk.shape[1]
    cb = bk.shape[2]
    g = lax.axis_index("gx")
    col = lax.axis_index("col")
    q = lax.axis_index("gy") * ncol + col

    def device(gg, qq):
        return {"gx": gg, "gy": qq // ncol, "col": qq % ncol}

    loads = [
        pltpu.make_async_copy(src, dst, load_sem.at[n])
        for n, (src, dst) in enumerate(
            (
                (vol_hbm, raw),
                (fk_hbm, fk),
                (fb_hbm, fb_ref),
                (dk_hbm, dk),
                (db_hbm, db_ref),
                (bb_hbm, bb_ref),
                (uk_hbm, uk),
                (ub_hbm, ub_ref),
            )
            + tuple((bk_hbm.at[pl.ds(3 * n, 3)], bk.at[pl.ds(3 * n, 3)]) for n in range(9))
        )
    ]
    loads[0].start()

    rim = 3

    def valid(gg, qq):
        ok = jnp.logical_and(gg >= 0, gg < ngx)
        return jnp.logical_and(ok, jnp.logical_and(qq >= 0, qq < nq))

    barrier = pltpu.get_barrier_semaphore()

    def greet(gg, qq):
        pl.semaphore_signal(barrier, inc=1, device_id=device(gg, qq), device_id_type=MESH)

    inner = 1 - 2 * col
    mate = q + inner
    beyond = q - inner
    has_beyond = valid(g, beyond)
    partners = 1 + has_beyond.astype(jnp.int32)
    for p in (g - 1, g + 1):
        there = valid(p, q)
        pl.when(there)(functools.partial(greet, p, q))
        partners += there.astype(jnp.int32)
    greet(g, mate)
    pl.when(has_beyond)(functools.partial(greet, g, beyond))

    loads[0].wait()
    for x in range(cx):
        brick[1 + cx * g + x, rim : rim + cy] = (
            raw[x].astype(F32).reshape(cy, depth, pair).astype(BF16)
        )
    pl.semaphore_wait(barrier, partners)

    def remote(src, dst, send, recv, gg, qq):
        return pltpu.make_async_remote_copy(
            src_ref=src,
            dst_ref=dst,
            send_sem=send,
            recv_sem=recv,
            device_id=device(gg, qq),
            device_id_type=MESH,
        )

    def layers(at):
        return pl.ds(1 + cx * at, cx)

    part = cx // PARTS

    def slab(at, n):
        return pl.ds(1 + cx * at + part * n, part)

    def block(source, to, n):
        ref = brick.at[slab(source, n), pl.ds(rim, cy)]
        return remote(ref, ref, block_send.at[to, n], block_recv.at[source, n], to, q)

    def rows_out(xs, b, count, send, recv, beside):
        src = jnp.where(b > 0, rim + cy - count, rim)
        dst = jnp.where(b > 0, rim - count, rim + cy)
        return remote(
            brick.at[xs, pl.ds(src, count)], brick.at[xs, pl.ds(dst, count)], send, recv, g, beside
        )

    def rows_in(xs, b, count, send, recv, beside):
        ref = brick.at[xs, pl.ds(jnp.where(b > 0, rim + cy, rim - count), count)]
        return remote(ref, ref, send, recv, g, beside)

    def inner_out(at):
        return rows_out(layers(at), inner, 1, inner_send.at[at], inner_recv.at[at], mate)

    def inner_in(at):
        return rows_in(layers(at), inner, 1, inner_send.at[at], inner_recv.at[at], mate)

    def outer_out(at, n):
        return rows_out(slab(at, n), -inner, rim, outer_send.at[at, n], outer_recv.at[at, n], beyond)

    def outer_in(at, n):
        return rows_in(slab(at, n), -inner, rim, outer_send.at[at, n], outer_recv.at[at, n], beyond)

    def others(visit, order):
        for d in order:
            for p in (g + d, g - d):
                pl.when(valid(p, q))(functools.partial(visit, p))

    near = tuple(range(1, ngx))

    def send(p):
        for n in range(PARTS):
            block(g, p, n).start()

    def tell(side):
        pl.semaphore_signal(
            word.at[side], inc=1, device_id=device(g + 2 * side - 1, q), device_id_type=MESH
        )

    between = jnp.logical_and(g > 0, g < ngx - 1)
    for side in (0, 1):
        pl.when(between)(functools.partial(tell, side))
    others(send, (1,))
    for n in range(PARTS):
        pl.when(has_beyond)(outer_out(g, n).start)
    inner_out(g).start()
    for d in range(2, ngx):
        for side in (0, 1):
            p = g + d if side == 0 else g - d

            @pl.when(valid(p, q))
            def _():
                pl.semaphore_wait(word.at[side], 1)
                send(p)
                pl.when(g > 0 if side == 0 else g < ngx - 1)(functools.partial(tell, side))


    for load in loads[1:]:
        load.start()
    half = cy // 2 + 2
    brick[0] = jnp.zeros_like(brick[0])
    brick[ngx * cx + 1] = jnp.zeros_like(brick[0])
    strip[0] = jnp.zeros_like(strip[0])
    strip[ngx * hx + 1] = jnp.zeros_like(strip[0])

    @pl.when(q == 0)
    def _():
        brick[1 : ngx * cx + 1, :rim] = jnp.zeros((ngx * cx, rim, depth, pair), BF16)

    @pl.when(q == nq - 1)
    def _():
        brick[1 : ngx * cx + 1, rim + cy :] = jnp.zeros((ngx * cx, rim, depth, pair), BF16)

    loads[1].wait()
    empty = jnp.zeros((chans, chans), BF16)
    for ij in range(9):
        f0, f1, f2 = fk[3 * ij], fk[3 * ij + 1], fk[3 * ij + 2]
        band[ij * pair : ij * pair + chans] = jnp.concatenate([f1, f0, empty, f2], axis=1)
        band[ij * pair + chans : (ij + 1) * pair] = jnp.concatenate([f2, f1, f0, empty], axis=1)

    def arrive(n, p):
        block(p, p, n).wait_recv()
        pl.when(has_beyond)(outer_out(p, n).start)
        if n == PARTS - 1:
            inner_out(p).start()

    for planes in (near[:1], near[1:]):
        for n in range(PARTS):
            others(functools.partial(arrive, n), planes)
    for load in loads[2:5]:
        load.wait()
    for p in range(ngx):
        inner_in(p).wait_recv()

    group = 2
    bunch = min(ngx, 4)

    def fine_rows(top, count, n):
        layer = group * cx * n
        pieces = [
            brick[pl.ds(layer + i, group * cx), pl.ds(top + j, count)].reshape(group * cx * count * depth, pair)
            for i in range(3)
            for j in range(3)
        ]
        prod = jnp.dot(jnp.concatenate(pieces, axis=1), band[...], preferred_element_type=F32)
        wing = prod[:, pair:]
        lane = lax.broadcasted_iota(jnp.int32, wing.shape, 1)
        fb = fb_ref[...]
        total = (
            prod[:, :pair]
            + jnp.where(lane < chans, shifted(wing, 1, depth), shifted(wing, -1, depth))
            + jnp.concatenate([fb, fb], axis=1)
        )
        fine = silu(total).astype(BF16).reshape(group * cx, count, depth, pair)
        fine_ref[pl.ds(layer, group * cx), pl.ds(top, count)] = fine

    def coarse_rows(top, count):
        @pl.loop(0, ngx // bunch)
        def _(n):
            fine = fine_ref[pl.ds(bunch * cx * n, bunch * cx), pl.ds(top, 2 * count)]
            cells = [
                jnp.concatenate(
                    [fine[2 * x + dx, 2 * y + dy] for dx in (0, 1) for dy in (0, 1)], axis=1
                )
                for x in range(bunch * hx)
                for y in range(count)
            ]
            coarse = jnp.dot(jnp.concatenate(cells, axis=0), dk[...], preferred_element_type=F32)
            coarse = silu(coarse + db_ref[...]).astype(BF16)
            strip[pl.ds(1 + bunch * hx * n, bunch * hx), pl.ds(top // 2, count)] = coarse.reshape(
                bunch * hx, count, depth, cd
            )

    early = jnp.where(inner > 0, 3, 2)
    late = jnp.where(inner > 0, 0, cy + 1)
    pl.loop(0, ngx // group)(functools.partial(fine_rows, early, cy - 1))
    coarse_rows(jnp.where(inner > 0, 4, 2), hy - 1)

    def share(sending):
        mine = jnp.where(inner > 0, hy, 1)
        rim_there = jnp.where(inner > 0, 0, hy + 1)
        rim_here = jnp.where(inner > 0, hy + 1, 0)
        every = pl.ds(1, ngx * hx)
        dst = strip.at[every, pl.ds(rim_there if sending else rim_here, 1)]
        src = strip.at[every, pl.ds(mine, 1)] if sending else dst
        return remote(src, dst, share_send, share_recv, g, mate)

    share(True).start()

    def steps(visit):
        @pl.loop(0, ngx - 1)
        def _(n):
            step = jnp.where(n % 2 == 1, (n + 1) // 2, -((n + 1) // 2))
            at = g // 2 + step
            pl.when(jnp.logical_and(at >= 0, at < ngx // 2))(functools.partial(visit, step, at))

    def late_rows(step, at):
        low = jnp.where(step > 0, 2 * at + 1, 2 * at - 1)
        high = jnp.where(step < 0, 2 * at, 2 * at + 2)
        for i in range(-1, 3):
            p = 2 * at + i
            new = jnp.logical_and(p >= low, p <= high)

            @pl.when(jnp.logical_and(has_beyond, jnp.logical_and(new, valid(p, q))))
            def _():
                for n in range(PARTS):
                    outer_in(p, n).wait_recv()

        fine_rows(late, 3, at)

    steps(late_rows)
    coarse_rows(jnp.where(inner > 0, 0, cy), 2)

    @pl.when(jnp.logical_not(has_beyond))
    def _():
        at_rim = pl.ds(jnp.where(inner > 0, 0, hy + 1), 1)
        strip[1 : ngx * hx + 1, at_rim] = jnp.zeros((ngx * hx, 1, depth, cd), BF16)

    share(False).wait_recv()
    for load in loads[5:]:
        load.wait()

    def swap(to, source):
        return remote(sent.at[to], back.at[source], swap_send.at[to], swap_recv.at[source], to, q)

    rows = hx * hy * depth

    @pl.loop(0, ngx // 2)
    def _(at):
        def taps(j, k):
            return [
                jnp.dot(
                    strip[pl.ds(2 * hx * at + i, 2 * hx), j : j + hy].reshape(2 * rows, cd),
                    bk[9 * i + 3 * j + k],
                    preferred_element_type=F32,
                )
                for i in range(3)
            ]

        for k in range(3):
            acc[k] = sum(taps(0, k) + taps(1, k) + taps(2, k))
        for i in range(2):
            p = 2 * at + i
            own = pl.ds(i * rows, rows)
            bottle = acc[1, own] + shifted(acc[0, own], 1, depth) + shifted(acc[2, own], -1, depth)
            sent[p] = silu(bottle + bb_ref[...]).astype(BF16)
            pl.when(p != g)(swap(p, g).start)

    ub = ub_ref[...]
    ub = jnp.concatenate([ub, ub], axis=1)
    lifted = jnp.dot(sent[g], uk[g], preferred_element_type=F32) + jnp.concatenate([ub] * 4, axis=1)
    for x in range(hx):
        for dx in (0, 1):
            for y in range(hy):
                at = (x * hy + y) * depth
                for dy in (0, 1):
                    c = (2 * dx + dy) * pair
                    base[at : at + depth, c : c + pair] = (
                        fine_ref[cx * g + 2 * x + dx, 2 + 2 * y + dy].astype(F32)
                        + lifted[at : at + depth, c : c + pair]
                    )
    for d in range(1, ngx - 1):
        source = lax.rem(g + d, ngx)
        swap(source, source).wait_recv()
        base[...] += jnp.dot(back[source], uk[source], preferred_element_type=F32)
    source = lax.rem(g + ngx - 1, ngx)
    swap(source, source).wait_recv()
    lifted = base[...] + jnp.dot(back[source], uk[source], preferred_element_type=F32)
    for x in range(hx):
        for dx in (0, 1):
            columns = []
            for y in range(hy):
                at = (x * hy + y) * depth
                for dy in (0, 1):
                    c = (2 * dx + dy) * pair
                    columns.append(lifted[at : at + depth, c : c + pair])
            out_ref[2 * x + dx] = jnp.stack(columns).reshape(cy, depth * pair).astype(BF16)

    def left(p):
        for n in range(PARTS):
            block(g, p, n).wait_send()
        swap(p, g).wait_send()

    others(left, near)
    for p in range(ngx):
        for n in range(PARTS):
            pl.when(has_beyond)(outer_out(p, n).wait_send)
        inner_out(p).wait_send()
    share(True).wait_send()


def local(
    sizes,
    volume,
    fine_kernel,
    fine_bias,
    down_kernel,
    down_bias,
    bottle_kernel,
    bottle_bias,
    up_kernel,
    up_bias,
):
    ngx = sizes[0]
    cx, cy, merged = volume.shape
    chans = fine_kernel.shape[1]
    pair = 2 * chans
    depth = merged // pair
    hx, hy = cx // 2, cy // 2
    cd = down_kernel.shape[1]
    cb = bottle_kernel.shape[2]
    cells = hx * hy * depth
    hbm = pl.BlockSpec(memory_space=pltpu.HBM)
    vmem = pl.BlockSpec(memory_space=pltpu.VMEM)
    dma = pltpu.SemaphoreType.DMA
    call = pl.pallas_call(
        functools.partial(body, sizes),
        out_shape=jax.ShapeDtypeStruct((cx, cy, merged), BF16),
        in_specs=[hbm] * 9,
        out_specs=vmem,
        scratch_shapes=[
            pltpu.VMEM(volume.shape, BF16),
            pltpu.VMEM((ngx * cx + 2, cy + 6, depth, pair), BF16),
            pltpu.VMEM(fine_kernel.shape, BF16),
            pltpu.VMEM((9 * pair, 2 * pair), BF16),
            pltpu.VMEM(down_kernel.shape, BF16),
            pltpu.VMEM(bottle_kernel.shape, BF16),
            pltpu.VMEM((ngx, cb, up_kernel.shape[1]), BF16),
            pltpu.VMEM((1, chans), F32),
            pltpu.VMEM((1, cd), F32),
            pltpu.VMEM((1, cb), F32),
            pltpu.VMEM((1, chans), F32),
            pltpu.VMEM((ngx * cx, cy + 4, depth, pair), BF16),
            pltpu.VMEM((ngx * hx + 2, hy + 2, depth, cd), BF16),
            pltpu.VMEM((3, 2 * cells, cb), F32),
            pltpu.VMEM((ngx, cells, cb), BF16),
            pltpu.VMEM((ngx, cells, cb), BF16),
            pltpu.SemaphoreType.REGULAR((2,)),
            dma((17,)),
            dma((ngx, PARTS)),
            dma((ngx, PARTS)),
            dma((ngx, PARTS)),
            dma((ngx, PARTS)),
            dma((ngx,)),
            dma((ngx,)),
            dma((ngx,)),
            dma((ngx,)),
            dma,
            dma,
            pltpu.VMEM((cells, up_kernel.shape[1]), F32),
        ],
        compiler_params=pltpu.CompilerParams(
            collective_id=0, has_side_effects=True, vmem_limit_bytes=52 << 20
        ),
    )
    arrays = (
        volume,
        fine_kernel,
        fine_bias.reshape(1, -1),
        down_kernel,
        down_bias.reshape(1, -1),
        bottle_kernel,
        bottle_bias.reshape(1, -1),
        up_kernel.reshape(ngx, cb, -1),
        up_bias.reshape(1, -1),
    )
    return call(*(pltpu.with_memory_space_constraint(a, pltpu.HBM) for a in arrays))


def solution(mesh):
    placed = (
        P(("groups", "gx"), ("gy", "col"), None),
        P(),
        P(),
        P(),
        P(),
        P(None, None, "gx"),
        P("gx"),
        P(),
        P(),
    )
    sizes = tuple(mesh.shape[name] for name in ("gx", "gy", "col"))
    return jax.shard_map(
        functools.partial(local, sizes),
        mesh=mesh,
        in_specs=placed,
        out_specs=P(("groups", "gx"), ("gy", "col"), None),
        check_vma=False,
    )
```
